256 devices in a mesh: rows: 256 (over z, x, y, core).
Axes of the slice: x: 4, y: 4, z: 8, core: 2. Of those that a mesh axis runs over, the one named last changes fastest.
Arguments:
- right_sides: float32 [131072, 2, 256], P('rows'), may hold values from -6 to 6
- order: int32 [131072], P('rows'), may hold values from 0 to 131071, as said below
- leaf_inverse: float32 [262144, 1024], P('rows')
- basis: float32 [8, 262144, 128], P(None, 'rows')
- capacitance: float32 [8, 256, 128, 128], P(None, 'rows'), as said below
Outputs:
- solution: float32 [131072, 2, 256], P('rows')
The draws below stay inside these ranges and needn't reach their ends.
Inputs may be any that keep to these rules, and one draw needn't show every extreme that they name: `order`: each aligned block of 512 entries holds every patch index of that block, j * 512 to (j + 1) * 512 - 1, exactly once. capacitance[k, d] is the same matrix for all d with the same d // 2 ** (k + 1).
All inputs are finite; a program needn't handle non-finite values.
Results may differ from the reference program's by a relative error of at most 0.0001.
Values sent between devices are 32-bit elements; how exact they have to be, the bound alone decides.
A program may use at most 128 MiB of HBM per device.

```python
import math
import jax
import jax.numpy as jnp
from jax import lax

PATCH_DEV = 512
COMP = 2
RANK = 64
RHS = 256
LEAF = 1024
PATCHES = 131072
ORDER = 262144
LEVELS = 8
N_ROWS = 256


def draw_order(key, part):
    scores = jax.random.randint(key, (N_ROWS, PATCH_DEV), 0, 1 << 20)
    within = jnp.arange(PATCH_DEV, dtype=jnp.int32)[None, :]
    distinct = scores * PATCH_DEV + within
    ranked = jnp.argsort(distinct, axis=1, stable=True).astype(jnp.int32)
    offsets = (jnp.arange(N_ROWS, dtype=jnp.int32) * PATCH_DEV)[:, None]
    return (ranked + offsets).reshape(PATCHES)


def rough(key, shape):
    return jax.random.normal(key, shape, jnp.float32)


def draw_leaf_inverse(key, part):
    first, second = jax.random.split(key)
    spread = rough(first, (ORDER, LEAF)) * (0.6 / math.sqrt(LEAF))
    diagonal = jnp.exp(jax.random.uniform(second, (ORDER, 1), jnp.float32, math.log(0.8), math.log(2.0)))
    row_local = jnp.arange(ORDER)[:, None] % LEAF
    columns = jnp.arange(LEAF)[None, :]
    return (spread + jnp.where(row_local == columns, diagonal, 0.0)).astype(jnp.float32)


def draw_basis(key, part):
    raw = rough(key, (LEVELS, ORDER, 2 * RANK))
    level = jnp.arange(LEVELS, dtype=jnp.float32)[:, None, None]
    columns = jnp.arange(2 * RANK)[None, None, :]
    right_scale = 1.0 / jnp.sqrt(LEAF * 2.0 ** level)
    scale = jnp.where(columns < RANK, 0.4 / math.sqrt(RANK), right_scale)
    return (raw * scale).astype(jnp.float32)


def draw_capacitance(key, part):
    first, second = jax.random.split(key)
    raw = rough(first, (LEVELS, N_ROWS, 2 * RANK, 2 * RANK)) * (0.5 / math.sqrt(2 * RANK))
    diagonal = jnp.exp(jax.random.uniform(second, (LEVELS, N_ROWS, 2 * RANK, 1), jnp.float32, math.log(0.5), math.log(1.5)))
    identity = jnp.arange(2 * RANK)[:, None] == jnp.arange(2 * RANK)[None, :]
    matrices = raw + jnp.where(identity, diagonal, 0.0)
    level = jnp.arange(LEVELS, dtype=jnp.int32)[:, None]
    device = jnp.arange(N_ROWS, dtype=jnp.int32)[None, :]
    leader = device >> level + 1 << level + 1
    return matrices[jnp.broadcast_to(level, leader.shape), leader].astype(jnp.float32)


def steps_of(stream_key, dims, cuts, smallest, largest):
    def one(axis_at, blocks):
        steps = jax.random.uniform(jax.random.fold_in(jax.random.fold_in(stream_key, 6), axis_at), (blocks,), jnp.float32, smallest / len(cuts), largest / len(cuts))
        return jnp.repeat(jnp.exp(steps), dims[axis_at] // blocks).reshape((-1,) + (1,) * (len(dims) - axis_at - 1))

    factor_of = one(*cuts[0])
    for cut in cuts[1:]:
        factor_of = factor_of * one(*cut)
    return factor_of


def centred(rng, dims, deviation, bound, shards=(), held_as=jnp.bfloat16):
    values = deviation * jax.random.normal(rng, dims, jnp.float32)
    if shards:
        values = values * steps_of(rng, dims, shards, -0.22, 0.18)
    return jnp.clip(values, -bound, bound).astype(held_as)


def setup_inputs(seed: int = 0) -> dict:
    arg_keys = jax.random.split(jax.random.key(seed), 6)
    return {
        "right_sides": centred(arg_keys[0], (PATCHES, COMP, RHS), 1.0, 6.0, ((0, 256),), jnp.float32),
        "order": draw_order(jax.random.fold_in(arg_keys[5], 71), 0),
        "leaf_inverse": draw_leaf_inverse(jax.random.fold_in(arg_keys[5], 71), 0),
        "basis": draw_basis(jax.random.fold_in(arg_keys[5], 71), 0),
        "capacitance": draw_capacitance(jax.random.fold_in(arg_keys[5], 71), 0),
    }


exact = lax.Precision.HIGHEST


def reference(right_sides, order, leaf_inverse, basis, capacitance):
    ordered = right_sides[order].reshape(N_ROWS, LEAF, RHS)
    blocks = leaf_inverse.reshape(N_ROWS, LEAF, LEAF)
    current = jnp.einsum("dij,djc->dic", blocks, ordered, precision=exact)
    for level in range(LEVELS):
        half = 2 ** level
        nodes = N_ROWS // (2 * half)
        parted = current.reshape(nodes, 2, half * LEAF, RHS)
        factors = basis[level].reshape(nodes, 2, half * LEAF, 2 * RANK)
        projected = jnp.einsum("nhrk,nhrc->nhkc", factors[..., RANK:], parted, precision=exact)
        coupled = projected[:, ::-1].reshape(nodes, 2 * RANK, RHS)
        inverse = capacitance[level, :: 2 * half]
        solved = jnp.einsum("nij,njc->nic", inverse, coupled, precision=exact).reshape(nodes, 2, RANK, RHS)
        parted = parted - jnp.einsum("nhrk,nhkc->nhrc", factors[..., :RANK], solved, precision=exact)
        current = parted.reshape(N_ROWS, LEAF, RHS)
    result = current.reshape(PATCHES, COMP, RHS)
    return jnp.zeros_like(right_sides).at[order].set(result)
```

```python
import functools

import jax
import jax.numpy as jnp
from jax import lax
from jax.experimental import pallas as pl
from jax.experimental.pallas import tpu as pltpu
from jax.sharding import PartitionSpec as P

F32 = jnp.float32
BF16 = jnp.bfloat16
MESH = pl.DeviceIdType.MESH
PACKED = (1, 2, 3, 4, 5, 6, 7, 0)
COPIES = 80
VMEM_BYTES = 56 * 1024 * 1024


def split(x):
    high = x.astype(BF16)
    return high, (x - high.astype(F32)).astype(BF16)


def mm(a, b, transposed=False):
    return lax.dot_general(
        a, b, (((1,), (1 if transposed else 0,)), ((), ())), preferred_element_type=F32
    )


def dot3(a, b, transposed=False):
    return mm(a[0], b[0], transposed) + (
        mm(a[0], b[1], transposed) + mm(a[1], b[0], transposed)
    )


def product(a, b, transposed=False):
    return dot3(split(a), split(b), transposed)


def lanes_of(x):
    return lax.broadcasted_iota(jnp.int32, x.shape, 1)


def swap(x):
    return pltpu.roll(x, 64, 1)


def join(left, right):
    return jnp.where(lanes_of(left) < 64, left, right)


def put(half, side):
    return half if side == 0 else swap(half)


def one_hot(order, first, count):
    rows = lax.broadcasted_iota(jnp.int32, (count, order.shape[1]), 0) + first
    return jnp.where(rows == order, 1.0, 0.0)


def solve_kernel(
    rhs, order, linv, basis, cap,
    field,
    rhs_v, linv_v, basis_v, cap_v,
    uh, ul, wh, wl, uth, utl, fth, ftl, gram,
    pick, xh, xl, gathered, oh, ol,
    qraw, q, q0_in, z0, a_in, za, zt0, qb, b_in, rr, x_in, c_in, z5s, z6s, dx, d_in, ztb,
    c1b, c3b, c5b, c6b, mp, mp_in, pk, pk_in, x4, z8, mx, mz,
    ssem, rsem, lsem,
):
    me = lax.axis_index("rows")
    core = lax.rem(me, 2)
    y = lax.rem(lax.div(me, 2), 4)
    x = lax.rem(lax.div(me, 8), 4)
    z = lax.div(me, 32)
    j = core * 4 + y
    plane = z * 32
    row = plane + x * 8
    cell = y * 2 + core

    def row_device(member):
        return row + lax.rem(member, 4) * 2 + lax.div(member, 4)

    row_members = [lax.rem(j + r, 8) for r in range(1, 8)]
    row_devices = [row_device(m) for m in row_members]
    y_members = [lax.rem(y + r, 4) for r in range(1, 4)]
    y_devices = [row + m * 2 + core for m in y_members]
    x_members = [lax.rem(x + r, 4) for r in range(1, 4)]
    x_devices = [plane + m * 8 + cell for m in x_members]
    z_members = [lax.rem(z + r, 8) for r in range(1, 8)]
    z_devices = [m * 32 + x * 8 + cell for m in z_members]
    other_core = row + y * 2 + (1 - core)

    used = [0]
    started = []

    def send(src, dst, device):
        at = used[0]
        used[0] += 1
        copy = pltpu.make_async_remote_copy(
            src_ref=src,
            dst_ref=dst,
            send_sem=ssem.at[at],
            recv_sem=rsem.at[at],
            device_id=(device,),
            device_id_type=MESH,
        )
        copy.start()
        started.append(copy)
        return copy

    def arrive(copies):
        for copy in copies:
            copy.wait_recv()

    def basis_load(c):
        rows = pl.ds(c * 128, 128)
        return pltpu.make_async_copy(basis.at[:, rows, :], basis_v.at[:, rows, :], lsem.at[c])

    def linv_load(c):
        rows = pl.ds(c * 128, 128)
        return pltpu.make_async_copy(linv.at[rows, :], linv_v.at[rows, :], lsem.at[8 + c])

    for c in range(8):
        basis_load(c).start()
    cap_load = pltpu.make_async_copy(cap, cap_v, lsem.at[16])
    cap_load.start()
    rhs_load = pltpu.make_async_copy(rhs, rhs_v, lsem.at[17])
    rhs_load.start()
    for c in range(8):
        linv_load(c).start()
    own = []
    for at, (level, buffer, node) in enumerate(
        ((1, c1b, lax.div(y, 2)), (3, c3b, lax.div(x, 2)), (5, c5b, lax.div(z, 2)), (6, c6b, lax.div(z, 4)))
    ):
        own.append(pltpu.make_async_copy(cap.at[level], buffer.at[node], lsem.at[18 + at]))
        own[-1].start()

    barrier = pltpu.get_barrier_semaphore()
    partners = row_devices + x_devices + z_devices
    for device in partners:
        pl.semaphore_signal(barrier, inc=1, device_id=(device,), device_id_type=MESH)

    def pack(c, carry):
        start = pl.multiple_of(c * 128, 128)
        rows = pl.ds(start, 128)
        basis_load(c).wait()
        for t in range(4):
            a = basis_v[PACKED[2 * t], rows, :]
            b = basis_v[PACKED[2 * t + 1], rows, :]
            u = join(a, swap(b))
            w = join(swap(a), b)
            cols = slice(128 * t, 128 * t + 128)
            uh[rows, cols], ul[rows, cols] = split(u)
            wh[rows, cols], wl[rows, cols] = split(w)
            uth[cols, rows], utl[cols, rows] = split(u.T)
        return carry

    lax.fori_loop(0, 8, pack, 0)

    pl.semaphore_wait(barrier, len(partners))
    cap_load.wait()
    for copy in own:
        copy.wait()
    c1_copies = [send(cap_v.at[1], c1b.at[lax.div(y, 2)], y_devices[1])]
    c3_copies = [send(cap_v.at[3], c3b.at[lax.div(x, 2)], x_devices[1])]
    c5_copies = [send(cap_v.at[5], c5b.at[lax.div(z, 2)], z_devices[r - 1]) for r in (2, 4, 6)]
    c6_copies = [send(cap_v.at[6], c6b.at[lax.div(z, 4)], z_devices[3])]

    for t, low in ((0, 0), (1, 128), (2, 256), (3, 0)):
        rows = slice(128 * t, 128 * t + 128)
        gram[rows, low:] = dot3((uth[rows, :], utl[rows, :]), (wh[:, low:], wl[:, low:]))

    mp[...] = join(swap(gram[0:32, 0:128]), gram[32:64, 0:128])
    for at, base in ((0, 128), (256, 192)):
        rows = slice(base, base + 64)
        pk[:, at : at + 128] = join(gram[rows, 384:512], gram[rows, 128:256])
        pk[:, at + 128 : at + 256] = gram[rows, 256:384]
    for at, base in ((512, 256), (640, 320)):
        rows = slice(base, base + 64)
        pk[:, at : at + 128] = join(gram[rows, 384:512], gram[rows, 256:384])
    mp_in[j] = mp[...]
    pk_in[j] = pk[pl.ds(pl.multiple_of(8 * j, 8), 8), :]
    mp_copies = [send(mp, mp_in.at[j], d) for d in row_devices]
    pk_copies = [
        send(pk.at[pl.ds(pl.multiple_of(8 * m, 8), 8), :], pk_in.at[j], d)
        for m, d in zip(row_members, row_devices)
    ]

    rhs_load.wait()
    local = order[...] - me * 512
    for b in range(4):
        pick[:, 128 * b : 128 * b + 128] = one_hot(local, 128 * b, 128).T.astype(BF16)
    for c in range(2):
        for half in range(2):
            cols = slice((2 * c + half) * 128, (2 * c + half) * 128 + 128)
            xh[:, cols], xl[:, cols] = split(rhs_v[pl.ds(2 * half + c, 512, stride=4), :])
    for source, target in ((xh, oh), (xl, ol)):
        for b in range(4):
            moved = mm(pick[128 * b : 128 * b + 128, :], source[...])
            for c in range(2):
                for half in range(2):
                    at = (2 * c + half) * 128
                    gathered[half, pl.ds(256 * b + c, 128, stride=2), :] = moved[:, at : at + 128]
        for half in range(2):
            target[:, 128 * half : 128 * half + 128] = gathered[half].astype(BF16)

    def leaf(c, carry):
        start = pl.multiple_of(c * 128, 128)
        rows = pl.ds(start, 128)
        linv_load(c).wait()
        value = dot3(split(linv_v[rows, :]), (oh[...], ol[...]))
        field[0, rows, :] = value[:, :128]
        field[1, rows, :] = value[:, 128:]
        fth[:, rows], ftl[:, rows] = split(value.T)
        return carry

    lax.fori_loop(0, 8, leaf, 0)

    arrive(pk_copies)
    total = pk_in[0]
    for m in range(1, 8):
        total = total + pk_in[m]
    x4[x] = total
    x4_copies = [send(x4.at[x], x4.at[x], d) for d in x_devices]

    for b in range(2):
        rows = slice(128 * b, 128 * b + 128)
        qraw[rows, :] = dot3((fth[rows, :], ftl[rows, :]), (wh[...], wl[...]))

    q0_copies = [send(qraw.at[:, pl.ds(384, 128)], q0_in, other_core)]

    own_rows = pl.ds(pl.multiple_of(8 * j, 8), 8)
    arrive(x4_copies)
    for m in range(4):
        mx[m, own_rows, :] = x4[m, :, 0:256]
    for h in range(2):
        mx[4 + h, own_rows, :] = x4[2 * h, :, 256:512] + x4[2 * h + 1, :, 256:512]
    zs = x4[0, :, 512:] + x4[1, :, 512:] + x4[2, :, 512:] + x4[3, :, 512:]
    z8[z] = zs
    z8_copies = [send(z8.at[z], z8.at[z], d) for d in z_devices]
    mxy_copies = [send(mx.at[:, own_rows, :], mx.at[:, own_rows, :], d) for d in y_devices]

    arrive(q0_copies)
    mine, others = qraw[:, 384:], q0_in[...]
    first = jnp.where(core == 0, mine, others)
    second = jnp.where(core == 0, others, mine)
    pair = join(swap(second), first)
    solved = product(pair, cap_v[0], True)
    solved = jnp.where(core == 0, swap(solved), solved)
    solved = jnp.where(lanes_of(solved) < 64, 0.0, solved)
    z0[...] = solved
    q[...] = qraw[...] - product(solved, gram[384:512, :])

    a_in[j] = q[pl.ds(pl.multiple_of(32 * j, 32), 32), 0:128]
    a_copies = [
        send(q.at[pl.ds(pl.multiple_of(32 * m, 32), 32), pl.ds(0, 128)], a_in.at[j], d)
        for m, d in zip(row_members, row_devices)
    ]
    arrive(z8_copies)
    for m in range(8):
        mz[m, own_rows, :] = z8[m, :, 0:128]
    for p in range(4):
        mz[8 + p, own_rows, :] = z8[2 * p, :, 128:] + z8[2 * p + 1, :, 128:]
    mzy_copies = [send(mz.at[:, own_rows, :], mz.at[:, own_rows, :], d) for d in y_devices]
    arrive(c1_copies)
    arrive(mp_copies)
    m12 = []
    for m in range(4):
        part = mp_in[m] + mp_in[4 + m]
        m12.append(jnp.concatenate([swap(part), part], 0))
    m12 = [jnp.concatenate(m12[2 * h : 2 * h + 2], 0) for h in range(2)]
    arrive(a_copies)
    parts = [a_in[m] + a_in[4 + m] for m in range(4)]
    z1 = [product(join(parts[2 * n + 1], swap(parts[2 * n])), c1b[n], True) for n in range(2)]
    left = [parts[2 * h] + parts[2 * h + 1] - product(z1[h], m12[h]) for h in range(2)]
    z2 = product(join(swap(left[1]), left[0]), cap_v[2], True)
    for m in range(4):
        za[m] = join(put(z1[m // 2], m % 2), put(z2, 1 - m // 2))
    own_cols = pl.ds(pl.multiple_of(32 * j, 32), 32)
    zt0[own_cols, :] = za[y]
    zt_copies = [
        send(za.at[lax.rem(m, 4)], zt0.at[own_cols, :], d)
        for m, d in zip(row_members, row_devices)
    ]
    arrive(mxy_copies)
    core_rows = pl.ds(pl.multiple_of(32 * core, 32), 32)
    mxc_copies = [send(mx.at[:, core_rows, :], mx.at[:, core_rows, :], other_core)]
    arrive(zt_copies)
    qb[...] = q[:, 128:] - product(zt0[...], gram[0:128, 128:])

    b_in[j] = qb[own_cols, :]
    b_copies = [
        send(qb.at[pl.ds(pl.multiple_of(32 * m, 32), 32), :], b_in.at[j], d)
        for m, d in zip(row_members, row_devices)
    ]
    arrive(mzy_copies)
    mzc_copies = [send(mz.at[:, core_rows, :], mz.at[:, core_rows, :], other_core)]
    arrive(b_copies)
    total = b_in[0]
    for m in range(1, 8):
        total = total + b_in[m]
    rr[...] = total
    x_rows = pl.ds(pl.multiple_of(8 * x, 8), 8)
    x_in[x] = rr[x_rows, :]
    x_copies = [
        send(rr.at[pl.ds(pl.multiple_of(8 * m, 8), 8), :], x_in.at[x], d)
        for m, d in zip(x_members, x_devices)
    ]
    arrive(c3_copies)
    arrive(mxc_copies)
    m3 = [jnp.concatenate([mx[2 * n], mx[2 * n + 1]], 0) for n in range(2)]
    m4 = jnp.concatenate([mx[4], mx[5]], 0)
    arrive(x_copies)
    low = [x_in[m, :, 0:128] for m in range(4)]
    z3 = [product(join(low[2 * n + 1], swap(low[2 * n])), c3b[n], True) for n in range(2)]
    y3 = [product(z3[n], m3[n]) for n in range(2)]
    left = [low[2 * h] + low[2 * h + 1] - y3[h][:, :128] for h in range(2)]
    z4 = product(join(swap(left[1]), left[0]), cap_v[4], True)
    taken = y3[0] + y3[1] + product(z4, m4)
    high = x_in[0, :, 128:] + x_in[1, :, 128:] + x_in[2, :, 128:] + x_in[3, :, 128:]
    high = jnp.concatenate([high[:, :128] - taken[:, 128:], high[:, 128:] - taken[:, :128]], 1)

    c_in[z] = high
    c_copies = [send(c_in.at[z], c_in.at[z], d) for d in z_devices]
    for m in range(4):
        dx[m, :, 0:128] = join(put(z3[m // 2], m % 2), put(z4, 1 - m // 2))
    arrive(c5_copies)
    arrive(c6_copies)
    arrive(mzc_copies)
    m5 = [jnp.concatenate([mz[2 * p], mz[2 * p + 1]], 0) for p in range(4)]
    m6 = [jnp.concatenate([mz[8 + 2 * n], mz[9 + 2 * n]], 0) for n in range(2)]
    arrive(c_copies)
    low = [c_in[m, :, 0:128] for m in range(8)]
    top = [c_in[m, :, 128:] for m in range(8)]
    z5 = [product(join(low[2 * p + 1], swap(low[2 * p])), c5b[p], True) for p in range(4)]
    y5 = [product(z5[p], m5[p]) for p in range(4)]
    left = [low[2 * p] + low[2 * p + 1] - y5[p] for p in range(4)]
    z6 = [product(join(swap(left[2 * n + 1]), left[2 * n]), c6b[n], True) for n in range(2)]
    y6 = [product(z6[n], m6[n]) for n in range(2)]
    left = []
    for h in range(2):
        value = top[4 * h] + top[4 * h + 1] + top[4 * h + 2] + top[4 * h + 3]
        left.append(value - y5[2 * h] - y5[2 * h + 1] - y6[h])
    z7 = product(join(left[1], swap(left[0])), cap_v[7], True)
    for p in range(4):
        z5s[p] = z5[p]
    for n in range(2):
        z6s[n] = z6[n]
    side5, side6, side7 = lax.rem(z, 2), lax.rem(lax.div(z, 2), 2), lax.div(z, 4)
    own5 = z5s[lax.div(z, 2)]
    own5 = jnp.where(side5 == 0, own5, swap(own5))
    own6 = z6s[lax.div(z, 4)]
    own6 = jnp.where(side6 == 0, swap(own6), own6)
    own7 = jnp.where(side7 == 0, z7, swap(z7))
    middle = join(own5, own6)
    for m in range(4):
        dx[m, :, 128:256] = middle
        dx[m, :, 256:384] = own7

    d_in[x_rows, :] = dx[x]
    d_copies = [send(dx.at[m], d_in.at[x_rows, :], d) for m, d in zip(x_members, x_devices)]
    arrive(d_copies)
    ztb[own_cols, :] = d_in[...]
    ztb_copies = [send(d_in, ztb.at[own_cols, :], d) for d in row_devices]
    arrive(ztb_copies)
    whole = jnp.concatenate([zt0[...], ztb[:, 0:256], join(ztb[:, 256:], z0[...])], 1)
    qh, ql = split(whole)
    fth[:, 0:512] = qh
    ftl[:, 0:512] = ql

    def update(c, carry):
        rows = pl.ds(pl.multiple_of(c * 128, 128), 128)
        taken = dot3((uh[rows, :], ul[rows, :]), (fth[:, 0:512], ftl[:, 0:512]), True)
        field[0, rows, :] = field[0, rows, :] - taken[:, :128]
        field[1, rows, :] = field[1, rows, :] - taken[:, 128:]
        return carry

    lax.fori_loop(0, 8, update, 0)
    for copy in started:
        copy.wait_send()
    assert used[0] == COPIES


def scatter_kernel(field, order, out):
    local = order[...] - lax.axis_index("rows") * 512
    picks = [one_hot(local, 128 * b, 128).astype(BF16) for b in range(4)]
    for c in range(2):
        value = jnp.concatenate([field[h, pl.ds(c, 512, stride=2), :] for h in range(2)], 1)
        high, low = split(value)
        rest = (value - high.astype(F32) - low.astype(F32)).astype(BF16)
        for b in range(4):
            moved = mm(picks[b], high) + (mm(picks[b], low) + mm(picks[b], rest))
            for h in range(2):
                out[pl.ds(512 * b + 2 * h + c, 128, stride=4), :] = moved[:, 128 * h : 128 * h + 128]


def shards(right_sides, order, leaf_inverse, basis, capacitance):
    rhs = right_sides.reshape(512, 2, 2, 128).transpose(0, 2, 1, 3).reshape(2048, 128)
    order = order.reshape(1, 512)
    any_ref = pl.BlockSpec(memory_space=pl.ANY)
    vmem_ref = pl.BlockSpec(memory_space=pltpu.VMEM)
    v = pltpu.VMEM
    field = pl.pallas_call(
        solve_kernel,
        out_shape=jax.ShapeDtypeStruct((2, 1024, 128), F32),
        in_specs=[any_ref, vmem_ref, any_ref, any_ref, any_ref],
        out_specs=vmem_ref,
        scratch_shapes=[
            v((2048, 128), F32), v((1024, 1024), F32), v((8, 1024, 128), F32), v((8, 128, 128), F32),
            v((1024, 512), BF16), v((1024, 512), BF16), v((1024, 512), BF16), v((1024, 512), BF16),
            v((512, 1024), BF16), v((512, 1024), BF16), v((256, 1024), BF16), v((256, 1024), BF16),
            v((512, 512), F32),
            v((512, 512), BF16), v((512, 512), BF16), v((512, 512), BF16), v((2, 1024, 128), F32),
            v((1024, 256), BF16), v((1024, 256), BF16),
            v((256, 512), F32), v((256, 512), F32), v((256, 128), F32), v((256, 128), F32),
            v((8, 32, 128), F32), v((4, 32, 128), F32), v((256, 128), F32), v((256, 384), F32),
            v((8, 32, 384), F32), v((32, 384), F32), v((4, 8, 384), F32), v((8, 8, 256), F32),
            v((4, 8, 128), F32), v((2, 8, 128), F32), v((4, 8, 384), F32), v((32, 384), F32),
            v((256, 384), F32),
            v((2, 128, 128), F32), v((2, 128, 128), F32), v((4, 128, 128), F32), v((2, 128, 128), F32),
            v((32, 128), F32), v((8, 32, 128), F32), v((64, 768), F32), v((8, 8, 768), F32),
            v((4, 8, 768), F32), v((8, 8, 256), F32),
            v((6, 64, 256), F32), v((12, 64, 128), F32),
            pltpu.SemaphoreType.DMA((COPIES,)), pltpu.SemaphoreType.DMA((COPIES,)),
            pltpu.SemaphoreType.DMA((22,)),
        ],
        compiler_params=pltpu.CompilerParams(
            collective_id=0, has_side_effects=True, vmem_limit_bytes=VMEM_BYTES
        ),
    )(rhs, order, leaf_inverse, basis, capacitance.reshape(8, 128, 128))
    out = pl.pallas_call(
        scatter_kernel,
        out_shape=jax.ShapeDtypeStruct((2048, 128), F32),
        in_specs=[vmem_ref, vmem_ref],
        out_specs=vmem_ref,
        compiler_params=pltpu.CompilerParams(vmem_limit_bytes=16 * 1024 * 1024),
    )(field, order)
    return out.reshape(512, 2, 2, 128).transpose(0, 2, 1, 3).reshape(512, 2, 256)


def solution(mesh):
    return jax.shard_map(
        shards,
        mesh=mesh,
        in_specs=(
            P("rows", None, None),
            P("rows"),
            P("rows", None),
            P(None, "rows", None),
            P(None, "rows", None, None),
        ),
        out_specs=P("rows", None, None),
        check_vma=False,
    )
```

```python
import functools

import jax
import jax.numpy as jnp
from jax import lax
from jax.experimental import pallas as pl
from jax.experimental.pallas import tpu as pltpu
from jax.sharding import PartitionSpec as P

F32 = jnp.float32
BF16 = jnp.bfloat16
MESH = pl.DeviceIdType.MESH
PACKED = (1, 2, 3, 4, 5, 6, 7, 0)
COPIES = 65
VMEM_BYTES = 56 * 1024 * 1024


def split(x):
    high = x.astype(BF16)
    return high, (x - high.astype(F32)).astype(BF16)


def mm(a, b, transposed=False):
    return lax.dot_general(
        a, b, (((1,), (1 if transposed else 0,)), ((), ())), preferred_element_type=F32
    )


def dot3(a, b, transposed=False):
    return mm(a[0], b[0], transposed) + (
        mm(a[0], b[1], transposed) + mm(a[1], b[0], transposed)
    )


def product(a, b, transposed=False):
    return dot3(split(a), split(b), transposed)


def lanes_of(x):
    return lax.broadcasted_iota(jnp.int32, x.shape, 1)


def swap(x):
    return pltpu.roll(x, 64, 1)


def join(left, right):
    return jnp.where(lanes_of(left) < 64, left, right)


def put(half, side):
    return half if side == 0 else swap(half)


def one_hot(order, first, count):
    rows = lax.broadcasted_iota(jnp.int32, (count, order.shape[1]), 0) + first
    return jnp.where(rows == order, 1.0, 0.0)


def solve_kernel(
    rhs, order, linv, basis, cap,
    out,
    rhs_v, linv_v, basis_v, cap_v,
    uh, ul, wh, wl, uth, utl, fth, ftl, gram,
    hot, pick, xh, xl, gathered, oh, ol, field,
    qraw, q_in, q, y_in, za, z0, rr, x_in, c_in, z5s, z6s, dx, d_in, zt0, ztb,
    c1b, c3b, c5b, c6b, g_in, g0, g12, g1, g2r, g2, pk, pk_in, x4, z8, mx, mz,
    ssem, rsem, lsem,
):
    me = lax.axis_index("rows")
    core = lax.rem(me, 2)
    y = lax.rem(lax.div(me, 2), 4)
    x = lax.rem(lax.div(me, 8), 4)
    z = lax.div(me, 32)
    j = core * 4 + y
    plane = z * 32
    row = plane + x * 8
    cell = y * 2 + core

    y_members = [lax.rem(y + r, 4) for r in range(1, 4)]
    y_devices = [row + m * 2 + core for m in y_members]
    x_members = [lax.rem(x + r, 4) for r in range(1, 4)]
    x_devices = [plane + m * 8 + cell for m in x_members]
    z_members = [lax.rem(z + r, 8) for r in range(1, 8)]
    z_devices = [m * 32 + x * 8 + cell for m in z_members]
    other_core = row + y * 2 + (1 - core)

    def rows_at(index, count):
        return pl.ds(pl.multiple_of(index * count, count), count)

    used = [0]
    started = []

    def send(src, dst, device):
        at = used[0]
        used[0] += 1
        copy = pltpu.make_async_remote_copy(
            src_ref=src,
            dst_ref=dst,
            send_sem=ssem.at[at],
            recv_sem=rsem.at[at],
            device_id=(device,),
            device_id_type=MESH,
        )
        copy.start()
        started.append(copy)
        return copy

    def arrive(copies):
        for copy in copies:
            copy.wait_recv()

    def basis_load(c):
        rows = pl.ds(c * 256, 256)
        return pltpu.make_async_copy(basis.at[:, rows, :], basis_v.at[:, rows, :], lsem.at[c])

    def linv_load(c):
        rows = pl.ds(c * 512, 512)
        return pltpu.make_async_copy(linv.at[rows, :], linv_v.at[rows, :], lsem.at[8 + c])

    for c in range(4):
        basis_load(c).start()
    cap_load = pltpu.make_async_copy(cap, cap_v, lsem.at[16])
    cap_load.start()
    rhs_load = pltpu.make_async_copy(rhs, rhs_v, lsem.at[17])
    rhs_load.start()
    for c in range(2):
        linv_load(c).start()
    own = []
    for at, (level, buffer, node) in enumerate(
        ((1, c1b, lax.div(y, 2)), (3, c3b, lax.div(x, 2)), (5, c5b, lax.div(z, 2)), (6, c6b, lax.div(z, 4)))
    ):
        own.append(pltpu.make_async_copy(cap.at[level], buffer.at[node], lsem.at[18 + at]))
        own[-1].start()

    barrier = pltpu.get_barrier_semaphore()
    partners = [other_core] + y_devices + x_devices + z_devices
    for device in partners:
        pl.semaphore_signal(barrier, inc=1, device_id=(device,), device_id_type=MESH)

    def pack(c, carry):
        rows = rows_at(c, 256)
        basis_load(c).wait()
        for t in range(4):
            a = basis_v[PACKED[2 * t], rows, :]
            b = basis_v[PACKED[2 * t + 1], rows, :]
            u = join(a, swap(b))
            w = join(swap(a), b)
            cols = slice(128 * t, 128 * t + 128)
            uh[rows, cols], ul[rows, cols] = split(u)
            wh[rows, cols], wl[rows, cols] = split(w)
            uth[cols, rows], utl[cols, rows] = split(u.T)
        return carry

    lax.fori_loop(0, 4, pack, 0)

    pl.semaphore_wait(barrier, len(partners))
    cap_load.wait()
    for copy in own:
        copy.wait()
    c1_copies = [send(cap_v.at[1], c1b.at[lax.div(y, 2)], y_devices[1])]

    g_copies = []
    for t, low in ((0, 0), (3, 0), (1, 128), (2, 256)):
        rows = slice(128 * t, 128 * t + 128)
        gram[rows, low:] = dot3((uth[rows, :], utl[rows, :]), (wh[:, low:], wl[:, low:]))
        if t == 3:
            g0[rows_at(core, 64), :] = gram[448:512, :]
            g0_copies = [send(gram.at[pl.ds(448, 64), :], g0.at[rows_at(core, 64), :], other_core)]
        else:
            at = gram.at[pl.ds(128 * t, 128), pl.ds(low, 512 - low)]
            to = g_in.at[pl.ds(128 * t, 128), pl.ds(low, 512 - low)]
            g_copies.append(send(at, to, other_core))
    c3_copies = [send(cap_v.at[3], c3b.at[lax.div(x, 2)], x_devices[1])]
    c5_copies = [send(cap_v.at[5], c5b.at[lax.div(z, 2)], z_devices[r - 1]) for r in (2, 4, 6)]
    c6_copies = [send(cap_v.at[6], c6b.at[lax.div(z, 4)], z_devices[3])]

    rhs_load.wait()
    local = order[...] - me * 512
    for b in range(4):
        block = one_hot(local, 128 * b, 128)
        hot[128 * b : 128 * b + 128, :] = block.astype(BF16)
        pick[:, 128 * b : 128 * b + 128] = block.T.astype(BF16)
    for c in range(2):
        for half in range(2):
            cols = slice((2 * c + half) * 128, (2 * c + half) * 128 + 128)
            xh[:, cols], xl[:, cols] = split(rhs_v[pl.ds(2 * half + c, 512, stride=4), :])

    arrive(g_copies[:1])
    for level in range(2):
        rows = pl.ds(pl.multiple_of(64 * level + 32 * core, 32), 32)
        tiles = [gram[rows, low : low + 128] + g_in[rows, low : low + 128] for low in (0, 128, 256, 384)]
        g12[level, :, 0:128] = join(tiles[3], tiles[0])
        g12[level, :, 128:256] = tiles[1]
        g12[level, :, 256:384] = tiles[2]
    core_rows = rows_at(core, 32)
    g1[y, core_rows, :] = g12[0]
    g2r[y, :, :] = g12[1]
    g1_copies = [send(g12.at[0], g1.at[y, core_rows, :], d) for d in y_devices]
    g2_copies = [send(g12.at[1], g2r.at[y], d) for d in y_devices]

    for source, target in ((xh, oh), (xl, ol)):
        for b in range(4):
            moved = mm(pick[128 * b : 128 * b + 128, :], source[...])
            for c in range(2):
                for half in range(2):
                    at = (2 * c + half) * 128
                    gathered[half, pl.ds(256 * b + c, 128, stride=2), :] = moved[:, at : at + 128]
        for half in range(2):
            target[:, 128 * half : 128 * half + 128] = gathered[half].astype(BF16)

    arrive(g_copies[1:])
    for at, base in ((0, 128), (256, 192)):
        rows = slice(base, base + 64)
        tiles = [gram[rows, low : low + 128] + g_in[rows, low : low + 128] for low in (128, 256, 384)]
        pk[:, at : at + 128] = join(tiles[2], tiles[0])
        pk[:, at + 128 : at + 256] = tiles[1]
    for at, base in ((512, 256), (640, 320)):
        rows = slice(base, base + 64)
        tiles = [gram[rows, low : low + 128] + g_in[rows, low : low + 128] for low in (256, 384)]
        pk[:, at : at + 128] = join(tiles[1], tiles[0])
    pk_in[y] = pk[rows_at(j, 8), :]
    pk_copies = [
        send(pk.at[rows_at(core * 4 + m, 8), :], pk_in.at[y], d) for m, d in zip(y_members, y_devices)
    ]

    def leaf(c, carry):
        rows = rows_at(c, 512)
        linv_load(c).wait()
        value = dot3(split(linv_v[rows, :]), (oh[...], ol[...]))
        field[0, rows, :] = value[:, :128]
        field[1, rows, :] = value[:, 128:]
        fth[:, rows], ftl[:, rows] = split(value.T)
        return carry

    lax.fori_loop(0, 2, leaf, 0)
    qraw[...] = dot3((fth[...], ftl[...]), (wh[...], wl[...]))

    own_half = rows_at(core, 128)
    q_copies = [send(qraw.at[rows_at(1 - core, 128), :], q_in, other_core)]
    own_rows = rows_at(j, 8)
    arrive(pk_copies)
    x4[x] = pk_in[0] + pk_in[1] + pk_in[2] + pk_in[3]
    x4_copies = [send(x4.at[x], x4.at[x], d) for d in x_devices]
    arrive(g0_copies)
    arrive(q_copies)
    mine, others = qraw[own_half, :], q_in[...]
    first = jnp.where(core == 0, mine[:, 384:], others[:, 384:])
    second = jnp.where(core == 0, others[:, 384:], mine[:, 384:])
    solved = product(join(swap(second), first), cap_v[0], True)
    q[...] = mine + others - product(solved, g0[...])

    y_in[y] = q[rows_at(y, 32), :]
    y_copies = [send(q.at[rows_at(m, 32), :], y_in.at[y], d) for m, d in zip(y_members, y_devices)]
    swapped = swap(solved)
    z0[0] = solved
    z0[1] = swapped
    z0_copies = [send(z0.at[core], z0.at[2], other_core)]
    arrive(g1_copies)
    arrive(g2_copies)
    g2[0, core_rows, :] = g2r[0] + g2r[1]
    g2[1, core_rows, :] = g2r[2] + g2r[3]
    g12c_copies = [
        send(g1.at[:, core_rows, :], g1.at[:, core_rows, :], other_core),
        send(g2.at[:, core_rows, :], g2.at[:, core_rows, :], other_core),
    ]
    arrive(x4_copies)
    for m in range(4):
        mx[m, own_rows, :] = x4[m, :, 0:256]
    for h in range(2):
        mx[4 + h, own_rows, :] = x4[2 * h, :, 256:512] + x4[2 * h + 1, :, 256:512]
    z8[z] = x4[0, :, 512:] + x4[1, :, 512:] + x4[2, :, 512:] + x4[3, :, 512:]
    z8_copies = [send(z8.at[z], z8.at[z], d) for d in z_devices]
    arrive(c1_copies)
    arrive(g12c_copies)
    m1 = [jnp.concatenate([g1[2 * n], g1[2 * n + 1]], 0) for n in range(2)]
    m2 = jnp.concatenate([g2[0], g2[1]], 0)
    arrive(y_copies)
    mxy_copies = [send(mx.at[:, own_rows, :], mx.at[:, own_rows, :], d) for d in y_devices]
    low = [y_in[m, :, 0:128] for m in range(4)]
    z1 = [product(join(low[2 * n + 1], swap(low[2 * n])), c1b[n], True) for n in range(2)]
    y1 = [product(z1[n], m1[n]) for n in range(2)]
    left = [low[2 * h] + low[2 * h + 1] - y1[h][:, :128] for h in range(2)]
    z2 = product(join(swap(left[1]), left[0]), cap_v[2], True)
    taken = y1[0] + y1[1] + product(z2, m2)
    high = y_in[0, :, 128:] + y_in[1, :, 128:] + y_in[2, :, 128:] + y_in[3, :, 128:]
    rr[:, 0:256] = high[:, 0:256] - taken[:, 128:]
    rr[:, 256:384] = high[:, 256:] - taken[:, :128]

    x_in[x] = rr[rows_at(x, 8), :]
    x_copies = [send(rr.at[rows_at(m, 8), :], x_in.at[x], d) for m, d in zip(x_members, x_devices)]
    for m in range(4):
        za[m] = join(put(z1[m // 2], m % 2), put(z2, 1 - m // 2))
    own_cols = rows_at(j, 32)
    zt0[own_cols, :] = za[y]
    za_copies = [send(za.at[m], zt0.at[own_cols, :], d) for m, d in zip(y_members, y_devices)]
    arrive(z8_copies)
    for m in range(8):
        mz[m, own_rows, :] = z8[m, :, 0:128]
    for p in range(4):
        mz[8 + p, own_rows, :] = z8[2 * p, :, 128:] + z8[2 * p + 1, :, 128:]
    mzy_copies = [send(mz.at[:, own_rows, :], mz.at[:, own_rows, :], d) for d in y_devices]
    arrive(c3_copies)
    arrive(mxy_copies)
    mxc_copies = [send(mx.at[:, core_rows, :], mx.at[:, core_rows, :], other_core)]
    arrive(mxc_copies)
    m3 = [jnp.concatenate([mx[2 * n], mx[2 * n + 1]], 0) for n in range(2)]
    m4 = jnp.concatenate([mx[4], mx[5]], 0)
    arrive(x_copies)
    low = [x_in[m, :, 0:128] for m in range(4)]
    z3 = [product(join(low[2 * n + 1], swap(low[2 * n])), c3b[n], True) for n in range(2)]
    y3 = [product(z3[n], m3[n]) for n in range(2)]
    left = [low[2 * h] + low[2 * h + 1] - y3[h][:, :128] for h in range(2)]
    z4 = product(join(swap(left[1]), left[0]), cap_v[4], True)
    taken = y3[0] + y3[1] + product(z4, m4)
    high = x_in[0, :, 128:] + x_in[1, :, 128:] + x_in[2, :, 128:] + x_in[3, :, 128:]
    high = jnp.concatenate([high[:, :128] - taken[:, 128:], high[:, 128:] - taken[:, :128]], 1)

    c_in[z] = high
    c_copies = [send(c_in.at[z], c_in.at[z], d) for d in z_devices]
    for m in range(4):
        dx[m, :, 0:128] = join(put(z3[m // 2], m % 2), put(z4, 1 - m // 2))
    arrive(mzy_copies)
    mzc_copies = [send(mz.at[:, core_rows, :], mz.at[:, core_rows, :], other_core)]
    arrive(za_copies)
    half_cols = rows_at(core, 128)
    zac_copies = [send(zt0.at[half_cols, :], zt0.at[half_cols, :], other_core)]
    arrive(c5_copies)
    arrive(c6_copies)
    arrive(mzc_copies)
    m5 = [jnp.concatenate([mz[2 * p], mz[2 * p + 1]], 0) for p in range(4)]
    m6 = [jnp.concatenate([mz[8 + 2 * n], mz[9 + 2 * n]], 0) for n in range(2)]
    arrive(c_copies)
    low = [c_in[m, :, 0:128] for m in range(8)]
    top = [c_in[m, :, 128:] for m in range(8)]
    z5 = [product(join(low[2 * p + 1], swap(low[2 * p])), c5b[p], True) for p in range(4)]
    y5 = [product(z5[p], m5[p]) for p in range(4)]
    left = [low[2 * p] + low[2 * p + 1] - y5[p] for p in range(4)]
    z6 = [product(join(swap(left[2 * n + 1]), left[2 * n]), c6b[n], True) for n in range(2)]
    y6 = [product(z6[n], m6[n]) for n in range(2)]
    left = []
    for h in range(2):
        value = top[4 * h] + top[4 * h + 1] + top[4 * h + 2] + top[4 * h + 3]
        left.append(value - y5[2 * h] - y5[2 * h + 1] - y6[h])
    z7 = product(join(left[1], swap(left[0])), cap_v[7], True)
    for p in range(4):
        z5s[p] = z5[p]
    for n in range(2):
        z6s[n] = z6[n]
    side5, side6, side7 = lax.rem(z, 2), lax.rem(lax.div(z, 2), 2), lax.div(z, 4)
    own5 = z5s[lax.div(z, 2)]
    own5 = jnp.where(side5 == 0, own5, swap(own5))
    own6 = z6s[lax.div(z, 4)]
    own6 = jnp.where(side6 == 0, swap(own6), own6)
    own7 = jnp.where(side7 == 0, z7, swap(z7))
    middle = join(own5, own6)
    for m in range(4):
        dx[m, :, 128:256] = middle
        dx[m, :, 256:384] = own7

    x_rows = rows_at(x, 8)
    d_in[x_rows, :] = dx[x]
    d_copies = [send(dx.at[m], d_in.at[x_rows, :], d) for m, d in zip(x_members, x_devices)]
    arrive(d_copies)
    ztb[own_cols, :] = d_in[...]
    ztb_copies = [send(d_in, ztb.at[own_cols, :], d) for d in y_devices]
    arrive(ztb_copies)
    ztbc_copies = [send(ztb.at[half_cols, :], ztb.at[half_cols, :], other_core)]
    arrive(z0_copies)
    arrive(zac_copies)
    arrive(ztbc_copies)
    near = z0[1 - core]
    far = z0[2]
    own0 = jnp.concatenate([jnp.where(core == 0, near, far), jnp.where(core == 0, far, near)], 0)
    whole = jnp.concatenate([zt0[...], ztb[:, 0:256], join(ztb[:, 256:], own0)], 1).T
    xh[:, 0:256], xl[:, 0:256] = split(whole)

    def update(c, carry):
        rows = rows_at(c, 512)
        taken = dot3((uh[rows, :], ul[rows, :]), (xh[:, 0:256], xl[:, 0:256]))
        field[0, rows, :] = field[0, rows, :] - taken[:, :128]
        field[1, rows, :] = field[1, rows, :] - taken[:, 128:]
        return carry

    lax.fori_loop(0, 2, update, 0)

    for c in range(2):
        value = jnp.concatenate([field[h, pl.ds(c, 512, stride=2), :] for h in range(2)], 1)
        xh[:, 256 * c : 256 * c + 256], xl[:, 256 * c : 256 * c + 256] = split(value)
    for b in range(4):
        rows = slice(128 * b, 128 * b + 128)
        moved = mm(hot[rows, :], xh[...]) + mm(hot[rows, :], xl[...])
        for c in range(2):
            for h in range(2):
                at = 256 * c + 128 * h
                out[pl.ds(512 * b + 2 * h + c, 128, stride=4), :] = moved[:, at : at + 128]
    for copy in started:
        copy.wait_send()
    assert used[0] == COPIES


def shards(right_sides, order, leaf_inverse, basis, capacitance):
    rhs = right_sides.reshape(512, 2, 2, 128).transpose(0, 2, 1, 3).reshape(2048, 128)
    order = order.reshape(1, 512)
    any_ref = pl.BlockSpec(memory_space=pl.ANY)
    vmem_ref = pl.BlockSpec(memory_space=pltpu.VMEM)
    f, h = (lambda *shape: pltpu.VMEM(shape, F32)), (lambda *shape: pltpu.VMEM(shape, BF16))
    out = pl.pallas_call(
        solve_kernel,
        out_shape=jax.ShapeDtypeStruct((2048, 128), F32),
        in_specs=[any_ref, vmem_ref, any_ref, any_ref, any_ref],
        out_specs=vmem_ref,
        scratch_shapes=[
            f(2048, 128), f(1024, 1024), f(8, 1024, 128), f(8, 128, 128),
            h(1024, 512), h(1024, 512), h(1024, 512), h(1024, 512),
            h(512, 1024), h(512, 1024), h(256, 1024), h(256, 1024), f(512, 512),
            h(512, 512), h(512, 512), h(512, 512), h(512, 512), f(2, 1024, 128),
            h(1024, 256), h(1024, 256), f(2, 1024, 128),
            f(256, 512), f(128, 512), f(128, 512), f(4, 32, 512), f(4, 32, 128), f(3, 128, 128),
            f(32, 384), f(4, 8, 384), f(8, 8, 256), f(4, 8, 128), f(2, 8, 128), f(4, 8, 384),
            f(32, 384), f(256, 128), f(256, 384),
            f(2, 128, 128), f(2, 128, 128), f(4, 128, 128), f(2, 128, 128),
            f(512, 512), f(128, 512), f(2, 32, 384), f(4, 64, 384), f(4, 32, 384), f(2, 64, 384),
            f(64, 768), f(4, 8, 768), f(4, 8, 768), f(8, 8, 256), f(6, 64, 256), f(12, 64, 128),
            pltpu.SemaphoreType.DMA((COPIES,)), pltpu.SemaphoreType.DMA((COPIES,)),
            pltpu.SemaphoreType.DMA((22,)),
        ],
        compiler_params=pltpu.CompilerParams(
            collective_id=0, has_side_effects=True, vmem_limit_bytes=VMEM_BYTES
        ),
    )(rhs, order, leaf_inverse, basis, capacitance.reshape(8, 128, 128))
    return out.reshape(512, 2, 2, 128).transpose(0, 2, 1, 3).reshape(512, 2, 256)


def solution(mesh):
    return jax.shard_map(
        shards,
        mesh=mesh,
        in_specs=(
            P("rows", None, None),
            P("rows"),
            P("rows", None),
            P(None, "rows", None),
            P(None, "rows", None, None),
        ),
        out_specs=P("rows", None, None),
        check_vma=False,
    )
```

```python
import functools

import jax
import jax.numpy as jnp
from jax import lax
from jax.experimental import pallas as pl
from jax.experimental.pallas import tpu as pltpu
from jax.sharding import PartitionSpec as P

F32 = jnp.float32
BF16 = jnp.bfloat16
MESH = pl.DeviceIdType.MESH
PACKED = (1, 2, 3, 4, 5, 6, 7, 0)
COPIES = 75
VMEM_BYTES = 58 * 1024 * 1024


def split(x):
    high = x.astype(BF16)
    return high, (x - high.astype(F32)).astype(BF16)


def mm(a, b, transposed=False):
    return lax.dot_general(
        a, b, (((1,), (1 if transposed else 0,)), ((), ())), preferred_element_type=F32
    )


def dot3(a, b, transposed=False):
    return mm(a[0], b[0], transposed) + (
        mm(a[0], b[1], transposed) + mm(a[1], b[0], transposed)
    )


def product(a, b, transposed=False):
    return dot3(split(a), split(b), transposed)


def lanes_of(x):
    return lax.broadcasted_iota(jnp.int32, x.shape, 1)


def swap(x):
    return pltpu.roll(x, 64, 1)


def join(left, right):
    return jnp.where(lanes_of(left) < 64, left, right)


def put(half, side):
    return half if side == 0 else swap(half)


def one_hot(order, first, count):
    rows = lax.broadcasted_iota(jnp.int32, (count, order.shape[1]), 0) + first
    return jnp.where(rows == order, 1.0, 0.0)


def solve_kernel(
    rhs, order, linv, basis, cap,
    field,
    rhs_v, linv_v, basis_v, cap_v,
    uh, ul, wh, wl, uth, utl, fth, ftl, gram,
    pick, xh, xl, gathered, oh, ol,
    qraw, q_in, q, y_in, za, z0, rr, x_in, c_in, z5s, z6s, dx, d_in, zt0, ztb,
    c1b, c3b, c5b, c6b, g_in, g0, g12, g1, g2r, g2, pk, pk_in, x4, z8, mx, mz,
    ssem, rsem, lsem,
):
    me = lax.axis_index("rows")
    core = lax.rem(me, 2)
    y = lax.rem(lax.div(me, 2), 4)
    x = lax.rem(lax.div(me, 8), 4)
    z = lax.div(me, 32)
    j = core * 4 + y
    plane = z * 32
    row = plane + x * 8
    cell = y * 2 + core

    y_members = [lax.rem(y + r, 4) for r in range(1, 4)]
    y_devices = [row + m * 2 + core for m in y_members]
    x_members = [lax.rem(x + r, 4) for r in range(1, 4)]
    x_devices = [plane + m * 8 + cell for m in x_members]
    z_members = [lax.rem(z + r, 8) for r in range(1, 8)]
    z_devices = [m * 32 + x * 8 + cell for m in z_members]
    other_core = row + y * 2 + (1 - core)

    def rows_at(index, count):
        return pl.ds(pl.multiple_of(index * count, count), count)

    used = [0]
    started = []

    def send(src, dst, device):
        at = used[0]
        used[0] += 1
        copy = pltpu.make_async_remote_copy(
            src_ref=src,
            dst_ref=dst,
            send_sem=ssem.at[at],
            recv_sem=rsem.at[at],
            device_id=(device,),
            device_id_type=MESH,
        )
        copy.start()
        started.append(copy)
        return copy

    def arrive(copies):
        for copy in copies:
            copy.wait_recv()

    def basis_load(c):
        rows = pl.ds(c * 256, 256)
        return pltpu.make_async_copy(basis.at[:, rows, :], basis_v.at[:, rows, :], lsem.at[c])

    def linv_load(c):
        rows = pl.ds(c * 512, 512)
        return pltpu.make_async_copy(linv.at[rows, :], linv_v.at[rows, :], lsem.at[8 + c])

    for c in range(4):
        basis_load(c).start()
    cap_load = pltpu.make_async_copy(cap, cap_v, lsem.at[16])
    cap_load.start()
    rhs_load = pltpu.make_async_copy(rhs, rhs_v, lsem.at[17])
    rhs_load.start()
    for c in range(2):
        linv_load(c).start()

    barrier = pltpu.get_barrier_semaphore()
    partners = [other_core] + y_devices + x_devices + z_devices
    for device in partners:
        pl.semaphore_signal(barrier, inc=1, device_id=(device,), device_id_type=MESH)

    def pack(c, carry):
        rows = rows_at(c, 256)
        basis_load(c).wait()
        for t in range(4):
            a = basis_v[PACKED[2 * t], rows, :]
            b = basis_v[PACKED[2 * t + 1], rows, :]
            u = join(a, swap(b))
            w = join(swap(a), b)
            cols = slice(128 * t, 128 * t + 128)
            uh[rows, cols], ul[rows, cols] = split(u)
            wh[rows, cols], wl[rows, cols] = split(w)
            uth[cols, rows], utl[cols, rows] = split(u.T)
        return carry

    lax.fori_loop(0, 4, pack, 0)

    g_copies = []
    for t, low in ((0, 0), (3, 0), (1, 128), (2, 256)):
        rows = slice(128 * t, 128 * t + 128)
        gram[rows, low:] = dot3((uth[rows, :], utl[rows, :]), (wh[:, low:], wl[:, low:]))
        if t == 0:
            pl.semaphore_wait(barrier, len(partners))
        if t == 3:
            g0[rows_at(core, 64), :] = gram[448:512, :]
            g0_copies = [send(gram.at[pl.ds(448, 64), :], g0.at[rows_at(core, 64), :], other_core)]
        else:
            at = gram.at[pl.ds(128 * t, 128), pl.ds(low, 512 - low)]
            to = g_in.at[pl.ds(128 * t, 128), pl.ds(low, 512 - low)]
            g_copies.append(send(at, to, other_core))
    cap_load.wait()
    halves, eighths = rows_at(core, 64), rows_at(j, 16)
    c1b[lax.div(y, 2)] = cap_v[1]
    c3b[lax.div(x, 2)] = cap_v[3]
    c5b[lax.div(z, 2), eighths, :] = cap_v[5, eighths, :]
    c6b[lax.div(z, 4), eighths, :] = cap_v[6, eighths, :]
    c1_copies = [send(cap_v.at[1, halves, :], c1b.at[lax.div(y, 2), halves, :], y_devices[1])]
    c3_copies = [send(cap_v.at[3, halves, :], c3b.at[lax.div(x, 2), halves, :], x_devices[1])]
    c5_copies = [
        send(cap_v.at[5, eighths, :], c5b.at[lax.div(z, 2), eighths, :], z_devices[r - 1]) for r in (2, 4, 6)
    ]
    c6_copies = [send(cap_v.at[6, eighths, :], c6b.at[lax.div(z, 4), eighths, :], z_devices[3])]

    rhs_load.wait()
    local = order[...] - me * 512
    for b in range(4):
        pick[:, 128 * b : 128 * b + 128] = one_hot(local, 128 * b, 128).T.astype(BF16)
    for c in range(2):
        for half in range(2):
            cols = slice((2 * c + half) * 128, (2 * c + half) * 128 + 128)
            xh[:, cols], xl[:, cols] = split(rhs_v[pl.ds(2 * half + c, 512, stride=4), :])

    arrive(g_copies[:1])
    for level in range(2):
        rows = pl.ds(pl.multiple_of(64 * level + 32 * core, 32), 32)
        tiles = [gram[rows, low : low + 128] + g_in[rows, low : low + 128] for low in (0, 128, 256, 384)]
        g12[level, :, 0:128] = join(tiles[3], tiles[0])
        g12[level, :, 128:256] = tiles[1]
        g12[level, :, 256:384] = tiles[2]
    core_rows = rows_at(core, 32)
    g1[y, core_rows, :] = g12[0]
    g2r[y, :, :] = g12[1]
    g1_copies = [send(g12.at[0], g1.at[y, core_rows, :], d) for d in y_devices]
    g2_copies = [send(g12.at[1], g2r.at[y], d) for d in y_devices]

    for source, target in ((xh, oh), (xl, ol)):
        for b in range(4):
            moved = mm(pick[128 * b : 128 * b + 128, :], source[...])
            for c in range(2):
                for half in range(2):
                    at = (2 * c + half) * 128
                    gathered[half, pl.ds(256 * b + c, 128, stride=2), :] = moved[:, at : at + 128]
        for half in range(2):
            target[:, 128 * half : 128 * half + 128] = gathered[half].astype(BF16)

    arrive(g_copies[1:])
    for at, base in ((0, 128), (256, 192)):
        rows = slice(base, base + 64)
        tiles = [gram[rows, low : low + 128] + g_in[rows, low : low + 128] for low in (128, 256, 384)]
        pk[:, at : at + 128] = join(tiles[2], tiles[0])
        pk[:, at + 128 : at + 256] = tiles[1]
    for at, base in ((512, 256), (640, 320)):
        rows = slice(base, base + 64)
        tiles = [gram[rows, low : low + 128] + g_in[rows, low : low + 128] for low in (256, 384)]
        pk[:, at : at + 128] = join(tiles[1], tiles[0])
    pk_in[y] = pk[rows_at(j, 8), :]
    pk_copies = [
        send(pk.at[rows_at(core * 4 + m, 8), :], pk_in.at[y], d) for m, d in zip(y_members, y_devices)
    ]

    def leaf(c, carry):
        rows = rows_at(c, 512)
        linv_load(c).wait()
        value = dot3(split(linv_v[rows, :]), (oh[...], ol[...]))
        field[0, rows, :] = value[:, :128]
        field[1, rows, :] = value[:, 128:]
        fth[:, rows], ftl[:, rows] = split(value.T)
        return carry

    lax.fori_loop(0, 2, leaf, 0)
    qraw[...] = dot3((fth[...], ftl[...]), (wh[...], wl[...]))

    own_half = rows_at(core, 128)
    q_copies = [send(qraw.at[rows_at(1 - core, 128), :], q_in, other_core)]
    own_rows = rows_at(j, 8)
    arrive(pk_copies)
    x4[x] = pk_in[0] + pk_in[1] + pk_in[2] + pk_in[3]
    x4_copies = [send(x4.at[x], x4.at[x], d) for d in x_devices]
    arrive(g0_copies)
    arrive(q_copies)
    mine, others = qraw[own_half, :], q_in[...]
    first = jnp.where(core == 0, mine[:, 384:], others[:, 384:])
    second = jnp.where(core == 0, others[:, 384:], mine[:, 384:])
    solved = product(join(swap(second), first), cap_v[0], True)
    q[...] = mine + others - product(solved, g0[...])

    y_in[y] = q[rows_at(y, 32), :]
    y_copies = [send(q.at[rows_at(m, 32), :], y_in.at[y], d) for m, d in zip(y_members, y_devices)]
    swapped = swap(solved)
    z0[0] = solved
    z0[1] = swapped
    z0_copies = [send(z0.at[core], z0.at[2], other_core)]
    arrive(g1_copies)
    arrive(g2_copies)
    g2[0, core_rows, :] = g2r[0] + g2r[1]
    g2[1, core_rows, :] = g2r[2] + g2r[3]
    arrive(c1_copies)
    far1 = 1 - lax.div(y, 2)
    g12c_copies = [
        send(c1b.at[far1, halves, :], c1b.at[far1, halves, :], other_core),
        send(g1.at[:, core_rows, :], g1.at[:, core_rows, :], other_core),
        send(g2.at[:, core_rows, :], g2.at[:, core_rows, :], other_core),
    ]
    arrive(x4_copies)
    for m in range(4):
        mx[m, own_rows, :] = x4[m, :, 0:256]
    for h in range(2):
        mx[4 + h, own_rows, :] = x4[2 * h, :, 256:512] + x4[2 * h + 1, :, 256:512]
    z8[z] = x4[0, :, 512:] + x4[1, :, 512:] + x4[2, :, 512:] + x4[3, :, 512:]
    z8_copies = [send(z8.at[z], z8.at[z], d) for d in z_devices]
    arrive(g12c_copies)
    m1 = [jnp.concatenate([g1[2 * n], g1[2 * n + 1]], 0) for n in range(2)]
    m2 = jnp.concatenate([g2[0], g2[1]], 0)
    arrive(y_copies)
    mxy_copies = [send(mx.at[:, own_rows, :], mx.at[:, own_rows, :], d) for d in y_devices]
    low = [y_in[m, :, 0:128] for m in range(4)]
    z1 = [product(join(low[2 * n + 1], swap(low[2 * n])), c1b[n], True) for n in range(2)]
    y1 = [product(z1[n], m1[n]) for n in range(2)]
    left = [low[2 * h] + low[2 * h + 1] - y1[h][:, :128] for h in range(2)]
    z2 = product(join(swap(left[1]), left[0]), cap_v[2], True)
    taken = y1[0] + y1[1] + product(z2, m2)
    high = y_in[0, :, 128:] + y_in[1, :, 128:] + y_in[2, :, 128:] + y_in[3, :, 128:]
    rr[:, 0:256] = high[:, 0:256] - taken[:, 128:]
    rr[:, 256:384] = high[:, 256:] - taken[:, :128]

    x_in[x] = rr[rows_at(x, 8), :]
    x_copies = [send(rr.at[rows_at(m, 8), :], x_in.at[x], d) for m, d in zip(x_members, x_devices)]
    for m in range(4):
        za[m] = join(put(z1[m // 2], m % 2), put(z2, 1 - m // 2))
    own_cols = rows_at(j, 32)
    zt0[own_cols, :] = za[y]
    za_copies = [send(za.at[m], zt0.at[own_cols, :], d) for m, d in zip(y_members, y_devices)]
    arrive(z8_copies)
    for m in range(8):
        mz[m, own_rows, :] = z8[m, :, 0:128]
    for p in range(4):
        mz[8 + p, own_rows, :] = z8[2 * p, :, 128:] + z8[2 * p + 1, :, 128:]
    mzy_copies = [send(mz.at[:, own_rows, :], mz.at[:, own_rows, :], d) for d in y_devices]
    arrive(c5_copies)
    arrive(c6_copies)
    mzy_copies += [send(c5b.at[:, eighths, :], c5b.at[:, eighths, :], d) for d in y_devices]
    mzy_copies += [send(c6b.at[:, eighths, :], c6b.at[:, eighths, :], d) for d in y_devices]
    arrive(c3_copies)
    arrive(mxy_copies)
    far3 = 1 - lax.div(x, 2)
    mxc_copies = [
        send(mx.at[:, core_rows, :], mx.at[:, core_rows, :], other_core),
        send(c3b.at[far3, halves, :], c3b.at[far3, halves, :], other_core),
    ]
    arrive(mxc_copies)
    m3 = [jnp.concatenate([mx[2 * n], mx[2 * n + 1]], 0) for n in range(2)]
    m4 = jnp.concatenate([mx[4], mx[5]], 0)
    arrive(x_copies)
    low = [x_in[m, :, 0:128] for m in range(4)]
    z3 = [product(join(low[2 * n + 1], swap(low[2 * n])), c3b[n], True) for n in range(2)]
    y3 = [product(z3[n], m3[n]) for n in range(2)]
    left = [low[2 * h] + low[2 * h + 1] - y3[h][:, :128] for h in range(2)]
    z4 = product(join(swap(left[1]), left[0]), cap_v[4], True)
    taken = y3[0] + y3[1] + product(z4, m4)
    high = x_in[0, :, 128:] + x_in[1, :, 128:] + x_in[2, :, 128:] + x_in[3, :, 128:]
    high = jnp.concatenate([high[:, :128] - taken[:, 128:], high[:, 128:] - taken[:, :128]], 1)

    c_in[z] = high
    c_copies = [send(c_in.at[z], c_in.at[z], d) for d in z_devices]
    for m in range(4):
        dx[m, :, 0:128] = join(put(z3[m // 2], m % 2), put(z4, 1 - m // 2))
    arrive(mzy_copies)
    mzc_copies = [
        send(mz.at[:, core_rows, :], mz.at[:, core_rows, :], other_core),
        send(c5b.at[:, halves, :], c5b.at[:, halves, :], other_core),
        send(c6b.at[:, halves, :], c6b.at[:, halves, :], other_core),
    ]
    arrive(za_copies)
    half_cols = rows_at(core, 128)
    zac_copies = [send(zt0.at[half_cols, :], zt0.at[half_cols, :], other_core)]
    arrive(mzc_copies)
    m5 = [jnp.concatenate([mz[2 * p], mz[2 * p + 1]], 0) for p in range(4)]
    m6 = [jnp.concatenate([mz[8 + 2 * n], mz[9 + 2 * n]], 0) for n in range(2)]
    arrive(c_copies)
    low = [c_in[m, :, 0:128] for m in range(8)]
    top = [c_in[m, :, 128:] for m in range(8)]
    z5 = [product(join(low[2 * p + 1], swap(low[2 * p])), c5b[p], True) for p in range(4)]
    y5 = [product(z5[p], m5[p]) for p in range(4)]
    left = [low[2 * p] + low[2 * p + 1] - y5[p] for p in range(4)]
    z6 = [product(join(swap(left[2 * n + 1]), left[2 * n]), c6b[n], True) for n in range(2)]
    y6 = [product(z6[n], m6[n]) for n in range(2)]
    left = []
    for h in range(2):
        value = top[4 * h] + top[4 * h + 1] + top[4 * h + 2] + top[4 * h + 3]
        left.append(value - y5[2 * h] - y5[2 * h + 1] - y6[h])
    z7 = product(join(left[1], swap(left[0])), cap_v[7], True)
    for p in range(4):
        z5s[p] = z5[p]
    for n in range(2):
        z6s[n] = z6[n]
    side5, side6, side7 = lax.rem(z, 2), lax.rem(lax.div(z, 2), 2), lax.div(z, 4)
    own5 = z5s[lax.div(z, 2)]
    own5 = jnp.where(side5 == 0, own5, swap(own5))
    own6 = z6s[lax.div(z, 4)]
    own6 = jnp.where(side6 == 0, swap(own6), own6)
    own7 = jnp.where(side7 == 0, z7, swap(z7))
    middle = join(own5, own6)
    for m in range(4):
        dx[m, :, 128:256] = middle
        dx[m, :, 256:384] = own7

    x_rows = rows_at(x, 8)
    d_in[x_rows, :] = dx[x]
    d_copies = [send(dx.at[m], d_in.at[x_rows, :], d) for m, d in zip(x_members, x_devices)]
    arrive(d_copies)
    ztb[own_cols, :] = d_in[...]
    ztb_copies = [send(d_in, ztb.at[own_cols, :], d) for d in y_devices]
    arrive(ztb_copies)
    ztbc_copies = [send(ztb.at[half_cols, :], ztb.at[half_cols, :], other_core)]
    arrive(z0_copies)
    arrive(zac_copies)
    arrive(ztbc_copies)
    near = z0[1 - core]
    far = z0[2]
    own0 = jnp.concatenate([jnp.where(core == 0, near, far), jnp.where(core == 0, far, near)], 0)
    whole = jnp.concatenate([zt0[...], ztb[:, 0:256], join(ztb[:, 256:], own0)], 1).T
    xh[:, 0:256], xl[:, 0:256] = split(whole)

    def update(c, carry):
        rows = rows_at(c, 512)
        taken = dot3((uh[rows, :], ul[rows, :]), (xh[:, 0:256], xl[:, 0:256]))
        field[0, rows, :] = field[0, rows, :] - taken[:, :128]
        field[1, rows, :] = field[1, rows, :] - taken[:, 128:]
        return carry

    lax.fori_loop(0, 2, update, 0)
    for copy in started:
        copy.wait_send()
    assert used[0] == COPIES


def scatter_kernel(field, order, out, high, low, done, sems):
    local = order[...] - lax.axis_index("rows") * 512
    for c in range(2):
        value = jnp.concatenate([field[h, pl.ds(c, 512, stride=2), :] for h in range(2)], 1)
        high[:, 256 * c : 256 * c + 256], low[:, 256 * c : 256 * c + 256] = split(value)
    copies = []
    for b in range(4):
        pick = one_hot(local, 128 * b, 128).astype(BF16)
        moved = mm(pick, high[...]) + mm(pick, low[...])
        for c in range(2):
            for h in range(2):
                at = 256 * c + 128 * h
                done[pl.ds(512 * b + 2 * h + c, 128, stride=4), :] = moved[:, at : at + 128]
        rows = pl.ds(512 * b, 512)
        copies.append(pltpu.make_async_copy(done.at[rows, :], out.at[rows, :], sems.at[b]))
        copies[-1].start()
    for copy in copies:
        copy.wait()


def shards(right_sides, order, leaf_inverse, basis, capacitance):
    rhs = right_sides.reshape(512, 2, 2, 128).transpose(0, 2, 1, 3).reshape(2048, 128)
    order = order.reshape(1, 512)
    any_ref = pl.BlockSpec(memory_space=pl.ANY)
    vmem_ref = pl.BlockSpec(memory_space=pltpu.VMEM)
    f, h = (lambda *shape: pltpu.VMEM(shape, F32)), (lambda *shape: pltpu.VMEM(shape, BF16))
    field = pl.pallas_call(
        solve_kernel,
        out_shape=pltpu.VMEM((2, 1024, 128), F32),
        in_specs=[any_ref, vmem_ref, any_ref, any_ref, any_ref],
        out_specs=vmem_ref,
        scratch_shapes=[
            f(2048, 128), f(1024, 1024), f(8, 1024, 128), f(8, 128, 128),
            h(1024, 512), h(1024, 512), h(1024, 512), h(1024, 512),
            h(512, 1024), h(512, 1024), h(256, 1024), h(256, 1024), f(512, 512),
            h(512, 512), h(512, 512), h(512, 512), f(2, 1024, 128),
            h(1024, 256), h(1024, 256),
            f(256, 512), f(128, 512), f(128, 512), f(4, 32, 512), f(4, 32, 128), f(3, 128, 128),
            f(32, 384), f(4, 8, 384), f(8, 8, 256), f(4, 8, 128), f(2, 8, 128), f(4, 8, 384),
            f(32, 384), f(256, 128), f(256, 384),
            f(2, 128, 128), f(2, 128, 128), f(4, 128, 128), f(2, 128, 128),
            f(512, 512), f(128, 512), f(2, 32, 384), f(4, 64, 384), f(4, 32, 384), f(2, 64, 384),
            f(64, 768), f(4, 8, 768), f(4, 8, 768), f(8, 8, 256), f(6, 64, 256), f(12, 64, 128),
            pltpu.SemaphoreType.DMA((COPIES,)), pltpu.SemaphoreType.DMA((COPIES,)),
            pltpu.SemaphoreType.DMA((22,)),
        ],
        compiler_params=pltpu.CompilerParams(
            collective_id=0, has_side_effects=True, vmem_limit_bytes=VMEM_BYTES
        ),
    )(rhs, order, leaf_inverse, basis, capacitance.reshape(8, 128, 128))
    out = pl.pallas_call(
        scatter_kernel,
        out_shape=jax.ShapeDtypeStruct((2048, 128), F32),
        in_specs=[vmem_ref, vmem_ref],
        out_specs=any_ref,
        scratch_shapes=[h(512, 512), h(512, 512), f(2048, 128), pltpu.SemaphoreType.DMA((4,))],
        compiler_params=pltpu.CompilerParams(vmem_limit_bytes=16 * 1024 * 1024),
    )(field, order)
    return out.reshape(512, 2, 2, 128).transpose(0, 2, 1, 3).reshape(512, 2, 256)


def solution(mesh):
    return jax.shard_map(
        shards,
        mesh=mesh,
        in_specs=(
            P("rows", None, None),
            P("rows"),
            P("rows", None),
            P(None, "rows", None),
            P(None, "rows", None, None),
        ),
        out_specs=P("rows", None, None),
        check_vma=False,
    )
```

```python
import functools

import jax
import jax.numpy as jnp
from jax import lax
from jax.experimental import pallas as pl
from jax.experimental.pallas import tpu as pltpu
from jax.sharding import PartitionSpec as P

F32 = jnp.float32
BF16 = jnp.bfloat16
MESH = pl.DeviceIdType.MESH
PACKED = (1, 2, 3, 4, 5, 6, 7, 0)
COPIES = 100
VMEM_BYTES = 58 * 1024 * 1024


def split(x):
    high = x.astype(BF16)
    return high, (x - high.astype(F32)).astype(BF16)


def mm(a, b, transposed=False):
    return lax.dot_general(
        a, b, (((1,), (1 if transposed else 0,)), ((), ())), preferred_element_type=F32
    )


def dot3(a, b, transposed=False):
    return mm(a[0], b[0], transposed) + (
        mm(a[0], b[1], transposed) + mm(a[1], b[0], transposed)
    )


def product(a, b, transposed=False):
    return dot3(split(a), split(b), transposed)


def lanes_of(x):
    return lax.broadcasted_iota(jnp.int32, x.shape, 1)


def swap(x):
    return pltpu.roll(x, 64, 1)


def join(left, right):
    return jnp.where(lanes_of(left) < 64, left, right)


def put(half, side):
    return half if side == 0 else swap(half)


def one_hot(order, first, count):
    rows = lax.broadcasted_iota(jnp.int32, (count, order.shape[1]), 0) + first
    return jnp.where(rows == order, 1.0, 0.0)


def solve_kernel(
    rhs, order, linv, basis, cap,
    field,
    rhs_v, linv_v, basis_v, cap_v,
    uh, ul, wh, wl, uth, utl, fth, ftl, gram,
    pick, xh, xl, gathered, oh, ol,
    qraw, q_in, q, y_in, za, z0, rr, x_in, c_in, z5s, z6s, dx, d_out, zt0, zt1, ztb,
    c1b, c3b, c5b, c6b, g_in, g0, g12, g1, g2r, g2, pk, pk_in, x4, z8, mx, mz,
    ssem, rsem, lsem,
):
    me = lax.axis_index("rows")
    core = lax.rem(me, 2)
    y = lax.rem(lax.div(me, 2), 4)
    x = lax.rem(lax.div(me, 8), 4)
    z = lax.div(me, 32)
    j = core * 4 + y
    plane = z * 32
    row = plane + x * 8
    cell = y * 2 + core

    y_members = [lax.rem(y + r, 4) for r in range(1, 4)]
    y_devices = [row + m * 2 + core for m in y_members]
    x_members = [lax.rem(x + r, 4) for r in range(1, 4)]
    x_devices = [plane + m * 8 + cell for m in x_members]
    z_members = [lax.rem(z + r, 8) for r in range(1, 8)]
    z_devices = [m * 32 + x * 8 + cell for m in z_members]
    other_core = row + y * 2 + (1 - core)
    plane_members = []
    for dy, dx_ in ((2, 2), (2, 1), (2, 3), (1, 2), (3, 2), (1, 1), (1, 3), (3, 1), (3, 3), (2, 0), (0, 2), (1, 0), (3, 0), (0, 1), (0, 3)):
        other_y, other_x = lax.rem(y + dy, 4), lax.rem(x + dx_, 4)
        plane_members.append((other_x, plane + other_x * 8 + other_y * 2 + core))

    def rows_at(index, count):
        return pl.ds(pl.multiple_of(index * count, count), count)

    used = [0]
    started = []

    def send(src, dst, device):
        at = used[0]
        used[0] += 1
        copy = pltpu.make_async_remote_copy(
            src_ref=src,
            dst_ref=dst,
            send_sem=ssem.at[at],
            recv_sem=rsem.at[at],
            device_id=(device,),
            device_id_type=MESH,
        )
        copy.start()
        started.append(copy)
        return copy

    def arrive(copies):
        for copy in copies:
            copy.wait_recv()

    def basis_load(c):
        rows = pl.ds(c * 256, 256)
        return pltpu.make_async_copy(basis.at[:, rows, :], basis_v.at[:, rows, :], lsem.at[c])

    def linv_load(c):
        rows = pl.ds(c * 512, 512)
        return pltpu.make_async_copy(linv.at[rows, :], linv_v.at[rows, :], lsem.at[8 + c])

    for c in range(4):
        basis_load(c).start()
    cap_load = pltpu.make_async_copy(cap, cap_v, lsem.at[16])
    cap_load.start()
    rhs_load = pltpu.make_async_copy(rhs, rhs_v, lsem.at[17])
    rhs_load.start()
    for c in range(2):
        linv_load(c).start()

    barrier = pltpu.get_barrier_semaphore()
    partners = [other_core] + [d for _, d in plane_members] + z_devices
    for device in partners:
        pl.semaphore_signal(barrier, inc=1, device_id=(device,), device_id_type=MESH)

    def pack(c, carry):
        rows = rows_at(c, 256)
        basis_load(c).wait()
        for t in range(4):
            a = basis_v[PACKED[2 * t], rows, :]
            b = basis_v[PACKED[2 * t + 1], rows, :]
            u = join(a, swap(b))
            w = join(swap(a), b)
            cols = slice(128 * t, 128 * t + 128)
            uh[rows, cols], ul[rows, cols] = split(u)
            wh[rows, cols], wl[rows, cols] = split(w)
            uth[cols, rows], utl[cols, rows] = split(u.T)
        return carry

    lax.fori_loop(0, 4, pack, 0)

    g_copies = []
    for t, low in ((0, 0), (3, 0), (1, 128), (2, 256)):
        rows = slice(128 * t, 128 * t + 128)
        gram[rows, low:] = dot3((uth[rows, :], utl[rows, :]), (wh[:, low:], wl[:, low:]))
        if t == 0:
            pl.semaphore_wait(barrier, len(partners))
        if t == 3:
            g0[rows_at(core, 64), :] = gram[448:512, :]
            g0_copies = [send(gram.at[pl.ds(448, 64), :], g0.at[rows_at(core, 64), :], other_core)]
        else:
            at = gram.at[pl.ds(128 * t, 128), pl.ds(low, 512 - low)]
            to = g_in.at[pl.ds(128 * t, 128), pl.ds(low, 512 - low)]
            g_copies.append(send(at, to, other_core))
    cap_load.wait()
    halves, eighths = rows_at(core, 64), rows_at(j, 16)
    c1b[lax.div(y, 2)] = cap_v[1]
    c3b[lax.div(x, 2)] = cap_v[3]
    c5b[lax.div(z, 2), eighths, :] = cap_v[5, eighths, :]
    c6b[lax.div(z, 4), eighths, :] = cap_v[6, eighths, :]
    c1_copies = [send(cap_v.at[1, halves, :], c1b.at[lax.div(y, 2), halves, :], y_devices[1])]
    c3_copies = [send(cap_v.at[3, halves, :], c3b.at[lax.div(x, 2), halves, :], x_devices[1])]
    c5_copies = [
        send(cap_v.at[5, eighths, :], c5b.at[lax.div(z, 2), eighths, :], z_devices[r - 1]) for r in (2, 4, 6)
    ]
    c6_copies = [send(cap_v.at[6, eighths, :], c6b.at[lax.div(z, 4), eighths, :], z_devices[3])]

    rhs_load.wait()
    local = order[...] - me * 512
    for b in range(4):
        pick[:, 128 * b : 128 * b + 128] = one_hot(local, 128 * b, 128).T.astype(BF16)
    for c in range(2):
        for half in range(2):
            cols = slice((2 * c + half) * 128, (2 * c + half) * 128 + 128)
            xh[:, cols], xl[:, cols] = split(rhs_v[pl.ds(2 * half + c, 512, stride=4), :])

    arrive(g_copies[:1])
    for level in range(2):
        rows = pl.ds(pl.multiple_of(64 * level + 32 * core, 32), 32)
        tiles = [gram[rows, low : low + 128] + g_in[rows, low : low + 128] for low in (0, 128, 256, 384)]
        g12[level, :, 0:128] = join(tiles[3], tiles[0])
        g12[level, :, 128:256] = tiles[1]
        g12[level, :, 256:384] = tiles[2]
    core_rows = rows_at(core, 32)
    g1[y, core_rows, :] = g12[0]
    g2r[y, :, :] = g12[1]
    g1_copies = [send(g12.at[0], g1.at[y, core_rows, :], d) for d in y_devices]
    g2_copies = [send(g12.at[1], g2r.at[y], d) for d in y_devices]

    arrive(g_copies[1:])
    for at, base in ((0, 128), (256, 192)):
        rows = slice(base, base + 64)
        tiles = [gram[rows, low : low + 128] + g_in[rows, low : low + 128] for low in (128, 256, 384)]
        pk[:, at : at + 128] = join(tiles[2], tiles[0])
        pk[:, at + 128 : at + 256] = tiles[1]
    for at, base in ((512, 256), (640, 320)):
        rows = slice(base, base + 64)
        tiles = [gram[rows, low : low + 128] + g_in[rows, low : low + 128] for low in (256, 384)]
        pk[:, at : at + 128] = join(tiles[1], tiles[0])
    pk_in[y] = pk[rows_at(j, 8), :]
    pk_copies = [
        send(pk.at[rows_at(core * 4 + m, 8), :], pk_in.at[y], d) for m, d in zip(y_members, y_devices)
    ]

    for source, target in ((xh, oh), (xl, ol)):
        for b in range(4):
            moved = mm(pick[128 * b : 128 * b + 128, :], source[...])
            for c in range(2):
                for half in range(2):
                    at = (2 * c + half) * 128
                    gathered[half, pl.ds(256 * b + c, 128, stride=2), :] = moved[:, at : at + 128]
        for half in range(2):
            target[:, 128 * half : 128 * half + 128] = gathered[half].astype(BF16)

    def leaf(c, carry):
        rows = rows_at(c, 512)
        linv_load(c).wait()
        value = dot3(split(linv_v[rows, :]), (oh[...], ol[...]))
        field[0, rows, :] = value[:, :128]
        field[1, rows, :] = value[:, 128:]
        fth[:, rows], ftl[:, rows] = split(value.T)
        return carry

    lax.fori_loop(0, 2, leaf, 0)
    qraw[...] = dot3((fth[...], ftl[...]), (wh[...], wl[...]))

    def update(cols, value):
        width = value.shape[1]
        xh[0:width, 0:256], xl[0:width, 0:256] = split(value.T)

        def step(c, carry):
            rows = rows_at(c, 512)
            taken = dot3((uh[rows, cols], ul[rows, cols]), (xh[0:width, 0:256], xl[0:width, 0:256]))
            field[0, rows, :] = field[0, rows, :] - taken[:, :128]
            field[1, rows, :] = field[1, rows, :] - taken[:, 128:]
            return carry

        lax.fori_loop(0, 2, step, 0)

    own_half = rows_at(core, 128)
    q_copies = [send(qraw.at[rows_at(1 - core, 128), :], q_in, other_core)]
    own_rows = rows_at(j, 8)
    arrive(pk_copies)
    x4[x] = pk_in[0] + pk_in[1] + pk_in[2] + pk_in[3]
    x4_copies = [send(x4.at[x], x4.at[x], d) for d in x_devices]
    arrive(g0_copies)
    arrive(q_copies)
    mine, others = qraw[own_half, :], q_in[...]
    first = jnp.where(core == 0, mine[:, 384:], others[:, 384:])
    second = jnp.where(core == 0, others[:, 384:], mine[:, 384:])
    solved = product(join(swap(second), first), cap_v[0], True)
    q[...] = mine + others - product(solved, g0[...])

    y_in[y] = q[rows_at(y, 32), :]
    y_copies = [send(q.at[rows_at(m, 32), :], y_in.at[y], d) for m, d in zip(y_members, y_devices)]
    swapped = swap(solved)
    z0[0] = solved
    z0[1] = swapped
    z0_copies = [send(z0.at[core], z0.at[2], other_core)]
    arrive(g1_copies)
    arrive(g2_copies)
    g2[0, core_rows, :] = g2r[0] + g2r[1]
    g2[1, core_rows, :] = g2r[2] + g2r[3]
    arrive(c1_copies)
    far1 = 1 - lax.div(y, 2)
    g12c_copies = [
        send(c1b.at[far1, halves, :], c1b.at[far1, halves, :], other_core),
        send(g1.at[:, core_rows, :], g1.at[:, core_rows, :], other_core),
        send(g2.at[:, core_rows, :], g2.at[:, core_rows, :], other_core),
    ]
    arrive(x4_copies)
    for m in range(4):
        mx[m, own_rows, :] = x4[m, :, 0:256]
    for h in range(2):
        mx[4 + h, own_rows, :] = x4[2 * h, :, 256:512] + x4[2 * h + 1, :, 256:512]
    z8[z] = x4[0, :, 512:] + x4[1, :, 512:] + x4[2, :, 512:] + x4[3, :, 512:]
    z8_copies = [send(z8.at[z], z8.at[z], d) for d in z_devices]
    arrive(g12c_copies)
    m1 = [jnp.concatenate([g1[2 * n], g1[2 * n + 1]], 0) for n in range(2)]
    m2 = jnp.concatenate([g2[0], g2[1]], 0)
    arrive(y_copies)
    mxy_copies = [send(mx.at[:, own_rows, :], mx.at[:, own_rows, :], d) for d in y_devices]
    low = [y_in[m, :, 0:128] for m in range(4)]
    z1 = [product(join(low[2 * n + 1], swap(low[2 * n])), c1b[n], True) for n in range(2)]
    y1 = [product(z1[n], m1[n]) for n in range(2)]
    left = [low[2 * h] + low[2 * h + 1] - y1[h][:, :128] for h in range(2)]
    z2 = product(join(swap(left[1]), left[0]), cap_v[2], True)
    taken = y1[0] + y1[1] + product(z2, m2)
    high = y_in[0, :, 128:] + y_in[1, :, 128:] + y_in[2, :, 128:] + y_in[3, :, 128:]
    rr[:, 0:256] = high[:, 0:256] - taken[:, 128:]
    rr[:, 256:384] = high[:, 256:] - taken[:, :128]

    x_in[x] = rr[rows_at(x, 8), :]
    x_copies = [send(rr.at[rows_at(m, 8), :], x_in.at[x], d) for m, d in zip(x_members, x_devices)]
    for m in range(4):
        za[m] = join(put(z1[m // 2], m % 2), put(z2, 1 - m // 2))
    own_cols = rows_at(j, 32)
    zt0[own_cols, :] = za[y]
    za_copies = [send(za.at[m], zt0.at[own_cols, :], d) for m, d in zip(y_members, y_devices)]
    arrive(z8_copies)
    for m in range(8):
        mz[m, own_rows, :] = z8[m, :, 0:128]
    for p in range(4):
        mz[8 + p, own_rows, :] = z8[2 * p, :, 128:] + z8[2 * p + 1, :, 128:]
    mzy_copies = [send(mz.at[:, own_rows, :], mz.at[:, own_rows, :], d) for d in y_devices]
    arrive(c5_copies)
    arrive(c6_copies)
    mzy_copies += [send(c5b.at[:, eighths, :], c5b.at[:, eighths, :], d) for d in y_devices]
    mzy_copies += [send(c6b.at[:, eighths, :], c6b.at[:, eighths, :], d) for d in y_devices]
    arrive(c3_copies)
    arrive(mxy_copies)
    far3 = 1 - lax.div(x, 2)
    mxc_copies = [
        send(mx.at[:, core_rows, :], mx.at[:, core_rows, :], other_core),
        send(c3b.at[far3, halves, :], c3b.at[far3, halves, :], other_core),
    ]
    arrive(mxc_copies)
    m3 = [jnp.concatenate([mx[2 * n], mx[2 * n + 1]], 0) for n in range(2)]
    m4 = jnp.concatenate([mx[4], mx[5]], 0)
    arrive(x_copies)
    low = [x_in[m, :, 0:128] for m in range(4)]
    z3 = [product(join(low[2 * n + 1], swap(low[2 * n])), c3b[n], True) for n in range(2)]
    y3 = [product(z3[n], m3[n]) for n in range(2)]
    left = [low[2 * h] + low[2 * h + 1] - y3[h][:, :128] for h in range(2)]
    z4 = product(join(swap(left[1]), left[0]), cap_v[4], True)
    taken = y3[0] + y3[1] + product(z4, m4)
    high = x_in[0, :, 128:] + x_in[1, :, 128:] + x_in[2, :, 128:] + x_in[3, :, 128:]
    high = jnp.concatenate([high[:, :128] - taken[:, 128:], high[:, 128:] - taken[:, :128]], 1)

    c_in[z] = high
    c_copies = [send(c_in.at[z], c_in.at[z], d) for d in z_devices]
    for m in range(4):
        dx[m] = join(put(z3[m // 2], m % 2), put(z4, 1 - m // 2))
    own_eight = pl.ds(pl.multiple_of(32 * j + 8 * x, 8), 8)
    zt1[own_eight, :] = dx[x]
    zt1_copies = [send(dx.at[m], zt1.at[own_eight, :], d) for m, d in plane_members]
    arrive(mzy_copies)
    mzc_copies = [
        send(mz.at[:, core_rows, :], mz.at[:, core_rows, :], other_core),
        send(c5b.at[:, halves, :], c5b.at[:, halves, :], other_core),
        send(c6b.at[:, halves, :], c6b.at[:, halves, :], other_core),
    ]
    arrive(za_copies)
    half_cols = rows_at(core, 128)
    zac_copies = [send(zt0.at[half_cols, :], zt0.at[half_cols, :], other_core)]
    arrive(mzc_copies)
    m5 = [jnp.concatenate([mz[2 * p], mz[2 * p + 1]], 0) for p in range(4)]
    m6 = [jnp.concatenate([mz[8 + 2 * n], mz[9 + 2 * n]], 0) for n in range(2)]
    arrive(z0_copies)
    arrive(zac_copies)
    near = z0[1 - core]
    far = z0[2]
    own0 = jnp.concatenate([jnp.where(core == 0, near, far), jnp.where(core == 0, far, near)], 0)
    update(slice(0, 128), zt0[...])
    update(slice(384, 512), join(jnp.zeros_like(own0), own0))
    arrive(c_copies)
    low = [c_in[m, :, 0:128] for m in range(8)]
    top = [c_in[m, :, 128:] for m in range(8)]
    z5 = [product(join(low[2 * p + 1], swap(low[2 * p])), c5b[p], True) for p in range(4)]
    y5 = [product(z5[p], m5[p]) for p in range(4)]
    left = [low[2 * p] + low[2 * p + 1] - y5[p] for p in range(4)]
    z6 = [product(join(swap(left[2 * n + 1]), left[2 * n]), c6b[n], True) for n in range(2)]
    y6 = [product(z6[n], m6[n]) for n in range(2)]
    left = []
    for h in range(2):
        value = top[4 * h] + top[4 * h + 1] + top[4 * h + 2] + top[4 * h + 3]
        left.append(value - y5[2 * h] - y5[2 * h + 1] - y6[h])
    z7 = product(join(left[1], swap(left[0])), cap_v[7], True)
    for p in range(4):
        z5s[p] = z5[p]
    for n in range(2):
        z6s[n] = z6[n]
    side5, side6, side7 = lax.rem(z, 2), lax.rem(lax.div(z, 2), 2), lax.div(z, 4)
    own5 = z5s[lax.div(z, 2)]
    own5 = jnp.where(side5 == 0, own5, swap(own5))
    own6 = z6s[lax.div(z, 4)]
    own6 = jnp.where(side6 == 0, swap(own6), own6)
    own7 = jnp.where(side7 == 0, z7, swap(z7))
    last = jnp.concatenate([join(own5, own6), join(own7, jnp.zeros_like(own7))], 1)

    d_out[...] = last
    ztb[own_eight, :] = last
    ztb_copies = [send(d_out, ztb.at[own_eight, :], d) for _, d in plane_members]
    arrive(zt1_copies)
    zt1c_copies = [send(zt1.at[half_cols, :], zt1.at[half_cols, :], other_core)]
    arrive(zt1c_copies)
    update(slice(128, 256), zt1[...])
    arrive(ztb_copies)
    ztbc_copies = [send(ztb.at[half_cols, :], ztb.at[half_cols, :], other_core)]
    arrive(ztbc_copies)
    update(slice(256, 512), ztb[...])
    for copy in started:
        copy.wait_send()
    assert used[0] == COPIES


def scatter_kernel(field, order, out, high, low, done, sems):
    local = order[...] - lax.axis_index("rows") * 512
    for c in range(2):
        value = jnp.concatenate([field[h, pl.ds(c, 512, stride=2), :] for h in range(2)], 1)
        high[:, 256 * c : 256 * c + 256], low[:, 256 * c : 256 * c + 256] = split(value)
    copies = []
    for b in range(4):
        pick = one_hot(local, 128 * b, 128).astype(BF16)
        moved = mm(pick, high[...]) + mm(pick, low[...])
        for c in range(2):
            for h in range(2):
                at = 256 * c + 128 * h
                done[pl.ds(512 * b + 2 * h + c, 128, stride=4), :] = moved[:, at : at + 128]
        rows = pl.ds(512 * b, 512)
        copies.append(pltpu.make_async_copy(done.at[rows, :], out.at[rows, :], sems.at[b]))
        copies[-1].start()
    for copy in copies:
        copy.wait()


def shards(right_sides, order, leaf_inverse, basis, capacitance):
    rhs = right_sides.reshape(512, 2, 2, 128).transpose(0, 2, 1, 3).reshape(2048, 128)
    order = order.reshape(1, 512)
    any_ref = pl.BlockSpec(memory_space=pl.ANY)
    vmem_ref = pl.BlockSpec(memory_space=pltpu.VMEM)
    f, h = (lambda *shape: pltpu.VMEM(shape, F32)), (lambda *shape: pltpu.VMEM(shape, BF16))
    field = pl.pallas_call(
        solve_kernel,
        out_shape=pltpu.VMEM((2, 1024, 128), F32),
        in_specs=[any_ref, vmem_ref, any_ref, any_ref, any_ref],
        out_specs=vmem_ref,
        scratch_shapes=[
            f(2048, 128), f(1024, 1024), f(8, 1024, 128), f(8, 128, 128),
            h(1024, 512), h(1024, 512), h(1024, 512), h(1024, 512),
            h(512, 1024), h(512, 1024), h(256, 1024), h(256, 1024), f(512, 512),
            h(512, 512), h(512, 512), h(512, 512), f(2, 1024, 128),
            h(1024, 256), h(1024, 256),
            f(256, 512), f(128, 512), f(128, 512), f(4, 32, 512), f(4, 32, 128), f(3, 128, 128),
            f(32, 384), f(4, 8, 384), f(8, 8, 256), f(4, 8, 128), f(2, 8, 128), f(4, 8, 128),
            f(8, 256), f(256, 128), f(256, 128), f(256, 256),
            f(2, 128, 128), f(2, 128, 128), f(4, 128, 128), f(2, 128, 128),
            f(512, 512), f(128, 512), f(2, 32, 384), f(4, 64, 384), f(4, 32, 384), f(2, 64, 384),
            f(64, 768), f(4, 8, 768), f(4, 8, 768), f(8, 8, 256), f(6, 64, 256), f(12, 64, 128),
            pltpu.SemaphoreType.DMA((COPIES,)), pltpu.SemaphoreType.DMA((COPIES,)),
            pltpu.SemaphoreType.DMA((22,)),
        ],
        compiler_params=pltpu.CompilerParams(
            collective_id=0, has_side_effects=True, vmem_limit_bytes=VMEM_BYTES
        ),
    )(rhs, order, leaf_inverse, basis, capacitance.reshape(8, 128, 128))
    out = pl.pallas_call(
        scatter_kernel,
        out_shape=jax.ShapeDtypeStruct((2048, 128), F32),
        in_specs=[vmem_ref, vmem_ref],
        out_specs=any_ref,
        scratch_shapes=[h(512, 512), h(512, 512), f(2048, 128), pltpu.SemaphoreType.DMA((4,))],
        compiler_params=pltpu.CompilerParams(vmem_limit_bytes=16 * 1024 * 1024),
    )(field, order)
    return out.reshape(512, 2, 2, 128).transpose(0, 2, 1, 3).reshape(512, 2, 256)


def solution(mesh):
    return jax.shard_map(
        shards,
        mesh=mesh,
        in_specs=(
            P("rows", None, None),
            P("rows"),
            P("rows", None),
            P(None, "rows", None),
            P(None, "rows", None, None),
        ),
        out_specs=P("rows", None, None),
        check_vma=False,
    )
```

```python
import functools

import jax
import jax.numpy as jnp
from jax import lax
from jax.experimental import pallas as pl
from jax.experimental.pallas import tpu as pltpu
from jax.sharding import PartitionSpec as P

F32 = jnp.float32
BF16 = jnp.bfloat16
MESH = pl.DeviceIdType.MESH
PACKED = (1, 2, 3, 4, 5, 6, 7, 0)
COPIES = 100
VMEM_BYTES = 58 * 1024 * 1024


def split(x):
    high = x.astype(BF16)
    return high, (x - high.astype(F32)).astype(BF16)


def mm(a, b, transposed=False):
    return lax.dot_general(
        a, b, (((1,), (1 if transposed else 0,)), ((), ())), preferred_element_type=F32
    )


def dot3(a, b, transposed=False):
    return mm(a[0], b[0], transposed) + (
        mm(a[0], b[1], transposed) + mm(a[1], b[0], transposed)
    )


def product(a, b, transposed=False):
    return dot3(split(a), split(b), transposed)


def lanes_of(x):
    return lax.broadcasted_iota(jnp.int32, x.shape, 1)


def swap(x):
    return pltpu.roll(x, 64, 1)


def join(left, right):
    return jnp.where(lanes_of(left) < 64, left, right)


def put(half, side):
    return half if side == 0 else swap(half)


def one_hot(order, first, count):
    rows = lax.broadcasted_iota(jnp.int32, (count, order.shape[1]), 0) + first
    return jnp.where(rows == order, 1.0, 0.0)


def solve_kernel(
    rhs, order, linv, basis, cap,
    field,
    rhs_v, linv_v, basis_v, cap_v,
    uh, ul, wh, wl, uth, utl, fth, ftl, gram,
    pick, xh, xl, gathered, oh, ol,
    qraw, q_in, q, y_in, za, z0, rr, x_in, c_in, z5s, z6s, dx, d_out, zt0, zt1, ztb,
    c1b, c3b, c5b, c6b, g_in, g0, g12, g1, g2r, g2, pk, pk_in, x4, z8, mx, mz,
    ssem, rsem, lsem,
):
    me = lax.axis_index("rows")
    core = lax.rem(me, 2)
    y = lax.rem(lax.div(me, 2), 4)
    x = lax.rem(lax.div(me, 8), 4)
    z = lax.div(me, 32)
    j = core * 4 + y
    plane = z * 32
    row = plane + x * 8
    cell = y * 2 + core

    y_members = [lax.rem(y + r, 4) for r in range(1, 4)]
    y_devices = [row + m * 2 + core for m in y_members]
    x_members = [lax.rem(x + r, 4) for r in range(1, 4)]
    x_devices = [plane + m * 8 + cell for m in x_members]
    z_members = [lax.rem(z + r, 8) for r in range(1, 8)]
    z_devices = [m * 32 + x * 8 + cell for m in z_members]
    other_core = row + y * 2 + (1 - core)
    plane_members = []
    for dy, dx_ in ((2, 2), (2, 1), (2, 3), (1, 2), (3, 2), (1, 1), (1, 3), (3, 1), (3, 3), (2, 0), (0, 2), (1, 0), (3, 0), (0, 1), (0, 3)):
        other_y, other_x = lax.rem(y + dy, 4), lax.rem(x + dx_, 4)
        plane_members.append((other_x, plane + other_x * 8 + other_y * 2 + core))

    def rows_at(index, count):
        return pl.ds(pl.multiple_of(index * count, count), count)

    used = [0]
    started = []

    def send(src, dst, device):
        at = used[0]
        used[0] += 1
        copy = pltpu.make_async_remote_copy(
            src_ref=src,
            dst_ref=dst,
            send_sem=ssem.at[at],
            recv_sem=rsem.at[at],
            device_id=(device,),
            device_id_type=MESH,
        )
        copy.start()
        started.append(copy)
        return copy

    def arrive(copies):
        for copy in copies:
            copy.wait_recv()

    def basis_load(c):
        rows = pl.ds(c * 256, 256)
        return pltpu.make_async_copy(basis.at[:, rows, :], basis_v.at[:, rows, :], lsem.at[c])

    def linv_load(c):
        rows = pl.ds(c * 512, 512)
        return pltpu.make_async_copy(linv.at[rows, :], linv_v.at[rows, :], lsem.at[8 + c])

    for c in range(4):
        basis_load(c).start()
    cap_load = pltpu.make_async_copy(cap, cap_v, lsem.at[16])
    cap_load.start()
    rhs_load = pltpu.make_async_copy(rhs, rhs_v, lsem.at[17])

    barrier = pltpu.get_barrier_semaphore()
    partners = [other_core] + [d for _, d in plane_members] + z_devices
    for device in partners:
        pl.semaphore_signal(barrier, inc=1, device_id=(device,), device_id_type=MESH)

    def pack(c, carry):
        rows = rows_at(c, 256)
        basis_load(c).wait()

        @pl.when(c == 2)
        def _():
            rhs_load.start()

        @pl.when(c == 3)
        def _():
            for part in range(2):
                linv_load(part).start()

        for t in range(4):
            a = basis_v[PACKED[2 * t], rows, :]
            b = basis_v[PACKED[2 * t + 1], rows, :]
            u = join(a, swap(b))
            w = join(swap(a), b)
            cols = slice(128 * t, 128 * t + 128)
            uh[rows, cols], ul[rows, cols] = split(u)
            wh[rows, cols], wl[rows, cols] = split(w)
            uth[cols, rows], utl[cols, rows] = split(u.T)
        return carry

    lax.fori_loop(0, 4, pack, 0)

    g_copies = []
    for t, low in ((0, 0), (3, 0), (1, 128), (2, 256)):
        rows = slice(128 * t, 128 * t + 128)
        gram[rows, low:] = dot3((uth[rows, :], utl[rows, :]), (wh[:, low:], wl[:, low:]))
        if t == 0:
            pl.semaphore_wait(barrier, len(partners))
        if t == 3:
            g0[rows_at(core, 64), :] = gram[448:512, :]
            g0_copies = [send(gram.at[pl.ds(448, 64), :], g0.at[rows_at(core, 64), :], other_core)]
        else:
            at = gram.at[pl.ds(128 * t, 128), pl.ds(low, 512 - low)]
            to = g_in.at[pl.ds(128 * t, 128), pl.ds(low, 512 - low)]
            g_copies.append(send(at, to, other_core))
    cap_load.wait()
    halves, eighths = rows_at(core, 64), rows_at(j, 16)
    c1b[lax.div(y, 2)] = cap_v[1]
    c3b[lax.div(x, 2)] = cap_v[3]
    c5b[lax.div(z, 2), eighths, :] = cap_v[5, eighths, :]
    c6b[lax.div(z, 4), eighths, :] = cap_v[6, eighths, :]
    c1_copies = [send(cap_v.at[1, halves, :], c1b.at[lax.div(y, 2), halves, :], y_devices[1])]
    c3_copies = [send(cap_v.at[3, halves, :], c3b.at[lax.div(x, 2), halves, :], x_devices[1])]
    c5_copies = [
        send(cap_v.at[5, eighths, :], c5b.at[lax.div(z, 2), eighths, :], z_devices[r - 1]) for r in (2, 4, 6)
    ]
    c6_copies = [send(cap_v.at[6, eighths, :], c6b.at[lax.div(z, 4), eighths, :], z_devices[3])]

    rhs_load.wait()
    local = order[...] - me * 512
    for b in range(4):
        pick[:, 128 * b : 128 * b + 128] = one_hot(local, 128 * b, 128).T.astype(BF16)
    for c in range(2):
        for half in range(2):
            cols = slice((2 * c + half) * 128, (2 * c + half) * 128 + 128)
            xh[:, cols], xl[:, cols] = split(rhs_v[pl.ds(2 * half + c, 512, stride=4), :])

    arrive(g_copies)
    for at, base in ((0, 128), (256, 192)):
        rows = slice(base, base + 64)
        tiles = [gram[rows, low : low + 128] + g_in[rows, low : low + 128] for low in (128, 256, 384)]
        pk[:, at : at + 128] = join(tiles[2], tiles[0])
        pk[:, at + 128 : at + 256] = tiles[1]
    for at, base in ((512, 256), (640, 320)):
        rows = slice(base, base + 64)
        tiles = [gram[rows, low : low + 128] + g_in[rows, low : low + 128] for low in (256, 384)]
        pk[:, at : at + 128] = join(tiles[1], tiles[0])
    pk_in[y] = pk[rows_at(j, 8), :]
    pk_copies = [
        send(pk.at[rows_at(core * 4 + m, 8), :], pk_in.at[y], d) for m, d in zip(y_members, y_devices)
    ]

    for level in range(2):
        rows = pl.ds(pl.multiple_of(64 * level + 32 * core, 32), 32)
        tiles = [gram[rows, low : low + 128] + g_in[rows, low : low + 128] for low in (0, 128, 256, 384)]
        g12[level, :, 0:128] = join(tiles[3], tiles[0])
        g12[level, :, 128:256] = tiles[1]
        g12[level, :, 256:384] = tiles[2]
    core_rows = rows_at(core, 32)
    g1[y, core_rows, :] = g12[0]
    g2r[y, :, :] = g12[1]
    g1_copies = [send(g12.at[0], g1.at[y, core_rows, :], d) for d in y_devices]
    g2_copies = [send(g12.at[1], g2r.at[y], d) for d in y_devices]

    for source, target in ((xh, oh), (xl, ol)):
        for b in range(4):
            moved = mm(pick[128 * b : 128 * b + 128, :], source[...])
            for c in range(2):
                for half in range(2):
                    at = (2 * c + half) * 128
                    gathered[half, pl.ds(256 * b + c, 128, stride=2), :] = moved[:, at : at + 128]
        for half in range(2):
            target[:, 128 * half : 128 * half + 128] = gathered[half].astype(BF16)

    def leaf(c, carry):
        rows = rows_at(c, 512)
        linv_load(c).wait()
        value = dot3(split(linv_v[rows, :]), (oh[...], ol[...]))
        field[0, rows, :] = value[:, :128]
        field[1, rows, :] = value[:, 128:]
        fth[:, rows], ftl[:, rows] = split(value.T)
        return carry

    lax.fori_loop(0, 2, leaf, 0)
    qraw[...] = dot3((fth[...], ftl[...]), (wh[...], wl[...]))

    def update(cols, value):
        width = value.shape[1]
        xh[0:width, 0:256], xl[0:width, 0:256] = split(value.T)

        def step(c, carry):
            rows = rows_at(c, 512)
            taken = dot3((uh[rows, cols], ul[rows, cols]), (xh[0:width, 0:256], xl[0:width, 0:256]))
            field[0, rows, :] = field[0, rows, :] - taken[:, :128]
            field[1, rows, :] = field[1, rows, :] - taken[:, 128:]
            return carry

        lax.fori_loop(0, 2, step, 0)

    own_half = rows_at(core, 128)
    q_copies = [send(qraw.at[rows_at(1 - core, 128), :], q_in, other_core)]
    own_rows = rows_at(j, 8)
    arrive(g0_copies)
    arrive(q_copies)
    arrive(pk_copies)
    x4[x] = pk_in[0] + pk_in[1] + pk_in[2] + pk_in[3]
    x4_copies = [send(x4.at[x], x4.at[x], d) for d in x_devices]
    mine, others = qraw[own_half, :], q_in[...]
    first = jnp.where(core == 0, mine[:, 384:], others[:, 384:])
    second = jnp.where(core == 0, others[:, 384:], mine[:, 384:])
    solved = product(join(swap(second), first), cap_v[0], True)
    q[...] = mine + others - product(solved, g0[...])

    y_in[y] = q[rows_at(y, 32), :]
    y_copies = [send(q.at[rows_at(m, 32), :], y_in.at[y], d) for m, d in zip(y_members, y_devices)]
    swapped = swap(solved)
    z0[0] = solved
    z0[1] = swapped
    z0_copies = [send(z0.at[core], z0.at[2], other_core)]
    arrive(g1_copies)
    arrive(g2_copies)
    g2[0, core_rows, :] = g2r[0] + g2r[1]
    g2[1, core_rows, :] = g2r[2] + g2r[3]
    arrive(c1_copies)
    far1 = 1 - lax.div(y, 2)
    g12c_copies = [
        send(c1b.at[far1, halves, :], c1b.at[far1, halves, :], other_core),
        send(g1.at[:, core_rows, :], g1.at[:, core_rows, :], other_core),
        send(g2.at[:, core_rows, :], g2.at[:, core_rows, :], other_core),
    ]
    arrive(x4_copies)
    for m in range(4):
        mx[m, own_rows, :] = x4[m, :, 0:256]
    for h in range(2):
        mx[4 + h, own_rows, :] = x4[2 * h, :, 256:512] + x4[2 * h + 1, :, 256:512]
    mxy_copies = [send(mx.at[:, own_rows, :], mx.at[:, own_rows, :], d) for d in y_devices]
    z8[z] = x4[0, :, 512:] + x4[1, :, 512:] + x4[2, :, 512:] + x4[3, :, 512:]
    z8_copies = [send(z8.at[z], z8.at[z], d) for d in z_devices]
    arrive(g12c_copies)
    m1 = [jnp.concatenate([g1[2 * n], g1[2 * n + 1]], 0) for n in range(2)]
    m2 = jnp.concatenate([g2[0], g2[1]], 0)
    arrive(y_copies)
    low = [y_in[m, :, 0:128] for m in range(4)]
    z1 = [product(join(low[2 * n + 1], swap(low[2 * n])), c1b[n], True) for n in range(2)]
    y1 = [product(z1[n], m1[n]) for n in range(2)]
    left = [low[2 * h] + low[2 * h + 1] - y1[h][:, :128] for h in range(2)]
    z2 = product(join(swap(left[1]), left[0]), cap_v[2], True)
    taken = y1[0] + y1[1] + product(z2, m2)
    high = y_in[0, :, 128:] + y_in[1, :, 128:] + y_in[2, :, 128:] + y_in[3, :, 128:]
    rr[:, 0:256] = high[:, 0:256] - taken[:, 128:]
    rr[:, 256:384] = high[:, 256:] - taken[:, :128]

    x_in[x] = rr[rows_at(x, 8), :]
    x_copies = [send(rr.at[rows_at(m, 8), :], x_in.at[x], d) for m, d in zip(x_members, x_devices)]
    for m in range(4):
        za[m] = join(put(z1[m // 2], m % 2), put(z2, 1 - m // 2))
    own_cols = rows_at(j, 32)
    zt0[own_cols, :] = za[y]
    za_copies = [send(za.at[m], zt0.at[own_cols, :], d) for m, d in zip(y_members, y_devices)]
    arrive(z8_copies)
    for m in range(8):
        mz[m, own_rows, :] = z8[m, :, 0:128]
    for p in range(4):
        mz[8 + p, own_rows, :] = z8[2 * p, :, 128:] + z8[2 * p + 1, :, 128:]
    mzy_copies = [send(mz.at[:, own_rows, :], mz.at[:, own_rows, :], d) for d in y_devices]
    arrive(c5_copies)
    arrive(c6_copies)
    mzy_copies += [send(c5b.at[:, eighths, :], c5b.at[:, eighths, :], d) for d in y_devices]
    mzy_copies += [send(c6b.at[:, eighths, :], c6b.at[:, eighths, :], d) for d in y_devices]
    arrive(c3_copies)
    arrive(mxy_copies)
    far3 = 1 - lax.div(x, 2)
    mxc_copies = [
        send(mx.at[:, core_rows, :], mx.at[:, core_rows, :], other_core),
        send(c3b.at[far3, halves, :], c3b.at[far3, halves, :], other_core),
    ]
    arrive(mxc_copies)
    m3 = [jnp.concatenate([mx[2 * n], mx[2 * n + 1]], 0) for n in range(2)]
    m4 = jnp.concatenate([mx[4], mx[5]], 0)
    arrive(x_copies)
    low = [x_in[m, :, 0:128] for m in range(4)]
    z3 = [product(join(low[2 * n + 1], swap(low[2 * n])), c3b[n], True) for n in range(2)]
    y3 = [product(z3[n], m3[n]) for n in range(2)]
    left = [low[2 * h] + low[2 * h + 1] - y3[h][:, :128] for h in range(2)]
    z4 = product(join(swap(left[1]), left[0]), cap_v[4], True)
    taken = y3[0] + y3[1] + product(z4, m4)
    high = x_in[0, :, 128:] + x_in[1, :, 128:] + x_in[2, :, 128:] + x_in[3, :, 128:]
    high = jnp.concatenate([high[:, :128] - taken[:, 128:], high[:, 128:] - taken[:, :128]], 1)

    c_in[z] = high
    c_copies = [send(c_in.at[z], c_in.at[z], d) for d in z_devices]
    for m in range(4):
        dx[m] = join(put(z3[m // 2], m % 2), put(z4, 1 - m // 2))
    own_eight = pl.ds(pl.multiple_of(32 * j + 8 * x, 8), 8)
    zt1[own_eight, :] = dx[x]
    zt1_copies = [send(dx.at[m], zt1.at[own_eight, :], d) for m, d in plane_members]
    arrive(mzy_copies)
    mzc_copies = [
        send(mz.at[:, core_rows, :], mz.at[:, core_rows, :], other_core),
        send(c5b.at[:, halves, :], c5b.at[:, halves, :], other_core),
        send(c6b.at[:, halves, :], c6b.at[:, halves, :], other_core),
    ]
    arrive(za_copies)
    half_cols = rows_at(core, 128)
    zac_copies = [send(zt0.at[half_cols, :], zt0.at[half_cols, :], other_core)]
    arrive(mzc_copies)
    m5 = [jnp.concatenate([mz[2 * p], mz[2 * p + 1]], 0) for p in range(4)]
    m6 = [jnp.concatenate([mz[8 + 2 * n], mz[9 + 2 * n]], 0) for n in range(2)]
    arrive(z0_copies)
    arrive(zac_copies)
    near = z0[1 - core]
    far = z0[2]
    own0 = jnp.concatenate([jnp.where(core == 0, near, far), jnp.where(core == 0, far, near)], 0)
    update(slice(0, 128), zt0[...])
    update(slice(384, 512), join(jnp.zeros_like(own0), own0))
    arrive(c_copies)
    low = [c_in[m, :, 0:128] for m in range(8)]
    top = [c_in[m, :, 128:] for m in range(8)]
    z5 = [product(join(low[2 * p + 1], swap(low[2 * p])), c5b[p], True) for p in range(4)]
    y5 = [product(z5[p], m5[p]) for p in range(4)]
    left = [low[2 * p] + low[2 * p + 1] - y5[p] for p in range(4)]
    z6 = [product(join(swap(left[2 * n + 1]), left[2 * n]), c6b[n], True) for n in range(2)]
    y6 = [product(z6[n], m6[n]) for n in range(2)]
    left = []
    for h in range(2):
        value = top[4 * h] + top[4 * h + 1] + top[4 * h + 2] + top[4 * h + 3]
        left.append(value - y5[2 * h] - y5[2 * h + 1] - y6[h])
    z7 = product(join(left[1], swap(left[0])), cap_v[7], True)
    for p in range(4):
        z5s[p] = z5[p]
    for n in range(2):
        z6s[n] = z6[n]
    side5, side6, side7 = lax.rem(z, 2), lax.rem(lax.div(z, 2), 2), lax.div(z, 4)
    own5 = z5s[lax.div(z, 2)]
    own5 = jnp.where(side5 == 0, own5, swap(own5))
    own6 = z6s[lax.div(z, 4)]
    own6 = jnp.where(side6 == 0, swap(own6), own6)
    own7 = jnp.where(side7 == 0, z7, swap(z7))
    last = jnp.concatenate([join(own5, own6), join(own7, jnp.zeros_like(own7))], 1)

    d_out[...] = last
    ztb[own_eight, :] = last
    ztb_copies = [send(d_out, ztb.at[own_eight, :], d) for _, d in plane_members]
    arrive(zt1_copies)
    zt1c_copies = [send(zt1.at[half_cols, :], zt1.at[half_cols, :], other_core)]
    arrive(zt1c_copies)
    update(slice(128, 256), zt1[...])
    arrive(ztb_copies)
    ztbc_copies = [send(ztb.at[half_cols, :], ztb.at[half_cols, :], other_core)]
    arrive(ztbc_copies)
    update(slice(256, 512), ztb[...])
    for copy in started:
        copy.wait_send()
    assert used[0] == COPIES


def scatter_kernel(field, order, out, high, low, done, sems):
    local = order[...] - lax.axis_index("rows") * 512
    for c in range(2):
        value = jnp.concatenate([field[h, pl.ds(c, 512, stride=2), :] for h in range(2)], 1)
        high[:, 256 * c : 256 * c + 256], low[:, 256 * c : 256 * c + 256] = split(value)
    copies = []
    for b in range(4):
        pick = one_hot(local, 128 * b, 128).astype(BF16)
        moved = mm(pick, high[...]) + mm(pick, low[...])
        for c in range(2):
            for h in range(2):
                at = 256 * c + 128 * h
                done[pl.ds(512 * b + 2 * h + c, 128, stride=4), :] = moved[:, at : at + 128]
        rows = pl.ds(512 * b, 512)
        copies.append(pltpu.make_async_copy(done.at[rows, :], out.at[rows, :], sems.at[b]))
        copies[-1].start()
    for copy in copies:
        copy.wait()


def shards(right_sides, order, leaf_inverse, basis, capacitance):
    rhs = right_sides.reshape(512, 2, 2, 128).transpose(0, 2, 1, 3).reshape(2048, 128)
    order = order.reshape(1, 512)
    any_ref = pl.BlockSpec(memory_space=pl.ANY)
    vmem_ref = pl.BlockSpec(memory_space=pltpu.VMEM)
    f, h = (lambda *shape: pltpu.VMEM(shape, F32)), (lambda *shape: pltpu.VMEM(shape, BF16))
    field = pl.pallas_call(
        solve_kernel,
        out_shape=pltpu.VMEM((2, 1024, 128), F32),
        in_specs=[any_ref, vmem_ref, any_ref, any_ref, any_ref],
        out_specs=vmem_ref,
        scratch_shapes=[
            f(2048, 128), f(1024, 1024), f(8, 1024, 128), f(8, 128, 128),
            h(1024, 512), h(1024, 512), h(1024, 512), h(1024, 512),
            h(512, 1024), h(512, 1024), h(256, 1024), h(256, 1024), f(512, 512),
            h(512, 512), h(512, 512), h(512, 512), f(2, 1024, 128),
            h(1024, 256), h(1024, 256),
            f(256, 512), f(128, 512), f(128, 512), f(4, 32, 512), f(4, 32, 128), f(3, 128, 128),
            f(32, 384), f(4, 8, 384), f(8, 8, 256), f(4, 8, 128), f(2, 8, 128), f(4, 8, 128),
            f(8, 256), f(256, 128), f(256, 128), f(256, 256),
            f(2, 128, 128), f(2, 128, 128), f(4, 128, 128), f(2, 128, 128),
            f(512, 512), f(128, 512), f(2, 32, 384), f(4, 64, 384), f(4, 32, 384), f(2, 64, 384),
            f(64, 768), f(4, 8, 768), f(4, 8, 768), f(8, 8, 256), f(6, 64, 256), f(12, 64, 128),
            pltpu.SemaphoreType.DMA((COPIES,)), pltpu.SemaphoreType.DMA((COPIES,)),
            pltpu.SemaphoreType.DMA((22,)),
        ],
        compiler_params=pltpu.CompilerParams(
            collective_id=0, has_side_effects=True, vmem_limit_bytes=VMEM_BYTES
        ),
    )(rhs, order, leaf_inverse, basis, capacitance.reshape(8, 128, 128))
    out = pl.pallas_call(
        scatter_kernel,
        out_shape=jax.ShapeDtypeStruct((2048, 128), F32),
        in_specs=[vmem_ref, vmem_ref],
        out_specs=any_ref,
        scratch_shapes=[h(512, 512), h(512, 512), f(2048, 128), pltpu.SemaphoreType.DMA((4,))],
        compiler_params=pltpu.CompilerParams(vmem_limit_bytes=16 * 1024 * 1024),
    )(field, order)
    return out.reshape(512, 2, 2, 128).transpose(0, 2, 1, 3).reshape(512, 2, 256)


def solution(mesh):
    return jax.shard_map(
        shards,
        mesh=mesh,
        in_specs=(
            P("rows", None, None),
            P("rows"),
            P("rows", None),
            P(None, "rows", None),
            P(None, "rows", None, None),
        ),
        out_specs=P("rows", None, None),
        check_vma=False,
    )
```

```python
import functools

import jax
import jax.numpy as jnp
from jax import lax
from jax.experimental import pallas as pl
from jax.experimental.pallas import tpu as pltpu
from jax.sharding import PartitionSpec as P

F32 = jnp.float32
BF16 = jnp.bfloat16
MESH = pl.DeviceIdType.MESH
PACKED = (1, 2, 3, 4, 5, 6, 7, 0)
COPIES = 100
VMEM_BYTES = 58 * 1024 * 1024


def split(x):
    high = x.astype(BF16)
    return high, (x - high.astype(F32)).astype(BF16)


def mm(a, b, transposed=False):
    return lax.dot_general(
        a, b, (((1,), (1 if transposed else 0,)), ((), ())), preferred_element_type=F32
    )


def dot3(a, b, transposed=False):
    return mm(a[0], b[0], transposed) + (
        mm(a[0], b[1], transposed) + mm(a[1], b[0], transposed)
    )


def product(a, b, transposed=False):
    return dot3(split(a), split(b), transposed)


def lanes_of(x):
    return lax.broadcasted_iota(jnp.int32, x.shape, 1)


def swap(x):
    return pltpu.roll(x, 64, 1)


def join(left, right):
    return jnp.where(lanes_of(left) < 64, left, right)


def put(half, side):
    return half if side == 0 else swap(half)


def one_hot(order, first, count):
    rows = lax.broadcasted_iota(jnp.int32, (count, order.shape[1]), 0) + first
    return jnp.where(rows == order, 1.0, 0.0)


def solve_kernel(
    rhs, order, linv, basis, cap,
    field,
    rhs_v, linv_v, basis_v, cap_v,
    uh, ul, wh, wl, uth, utl, fth, ftl, gram,
    pick, xh, xl, gathered, oh, ol,
    qraw, q_in, q, y_in, za, z0, rr, x_in, c_in, z5s, z6s, dx, d_out, zt0, zt1, ztb,
    c1b, c3b, c5b, c6b, g_in, g0, g12, g1, g2r, g2, pk, pk_in, x4, z8, mx, mz,
    ssem, rsem, lsem,
):
    me = lax.axis_index("rows")
    core = lax.rem(me, 2)
    y = lax.rem(lax.div(me, 2), 4)
    x = lax.rem(lax.div(me, 8), 4)
    z = lax.div(me, 32)
    j = core * 4 + y
    plane = z * 32
    row = plane + x * 8
    cell = y * 2 + core

    y_members = [lax.rem(y + r, 4) for r in (2, 1, 3)]
    y_devices = [row + m * 2 + core for m in y_members]
    x_members = [lax.rem(x + r, 4) for r in (2, 1, 3)]
    x_devices = [plane + m * 8 + cell for m in x_members]
    z_members = [lax.rem(z + r, 8) for r in (4, 3, 5, 2, 6, 1, 7)]
    z_devices = [m * 32 + x * 8 + cell for m in z_members]
    other_core = row + y * 2 + (1 - core)
    plane_members = []
    for dy, dx_ in ((2, 2), (2, 1), (2, 3), (1, 2), (3, 2), (1, 1), (1, 3), (3, 1), (3, 3), (2, 0), (0, 2), (1, 0), (3, 0), (0, 1), (0, 3)):
        other_y, other_x = lax.rem(y + dy, 4), lax.rem(x + dx_, 4)
        plane_members.append((other_x, plane + other_x * 8 + other_y * 2 + core))

    def rows_at(index, count):
        return pl.ds(pl.multiple_of(index * count, count), count)

    used = [0]
    started = []

    def send(src, dst, device):
        at = used[0]
        used[0] += 1
        copy = pltpu.make_async_remote_copy(
            src_ref=src,
            dst_ref=dst,
            send_sem=ssem.at[at],
            recv_sem=rsem.at[at],
            device_id=(device,),
            device_id_type=MESH,
        )
        copy.start()
        started.append(copy)
        return copy

    def arrive(copies):
        for copy in copies:
            copy.wait_recv()

    def basis_load(c):
        rows = pl.ds(c * 256, 256)
        return pltpu.make_async_copy(basis.at[:, rows, :], basis_v.at[:, rows, :], lsem.at[c])

    def linv_load(c):
        rows = pl.ds(c * 512, 512)
        return pltpu.make_async_copy(linv.at[rows, :], linv_v.at[rows, :], lsem.at[8 + c])

    rhs_load = pltpu.make_async_copy(rhs, rhs_v, lsem.at[17])
    rhs_load.start()
    for c in range(4):
        basis_load(c).start()
    cap_load = pltpu.make_async_copy(cap, cap_v, lsem.at[16])
    cap_load.start()

    barrier = pltpu.get_barrier_semaphore()
    partners = [other_core] + [d for _, d in plane_members] + z_devices
    for device in partners:
        pl.semaphore_signal(barrier, inc=1, device_id=(device,), device_id_type=MESH)

    rhs_load.wait()
    local = order[...] - me * 512
    for b in range(4):
        pick[:, 128 * b : 128 * b + 128] = one_hot(local, 128 * b, 128).T.astype(BF16)
    for c in range(2):
        for half in range(2):
            cols = slice((2 * c + half) * 128, (2 * c + half) * 128 + 128)
            xh[:, cols], xl[:, cols] = split(rhs_v[pl.ds(2 * half + c, 512, stride=4), :])
    for source, target in ((xh, oh), (xl, ol)):
        for b in range(4):
            moved = mm(pick[128 * b : 128 * b + 128, :], source[...])
            for c in range(2):
                for half in range(2):
                    at = (2 * c + half) * 128
                    gathered[half, pl.ds(256 * b + c, 128, stride=2), :] = moved[:, at : at + 128]
        for half in range(2):
            target[:, 128 * half : 128 * half + 128] = gathered[half].astype(BF16)

    def pack(c, carry):
        rows = rows_at(c, 256)
        basis_load(c).wait()

        @pl.when(c == 2)
        def _():
            for part in range(2):
                linv_load(part).start()

        for t in range(4):
            a = basis_v[PACKED[2 * t], rows, :]
            b = basis_v[PACKED[2 * t + 1], rows, :]
            u = join(a, swap(b))
            w = join(swap(a), b)
            cols = slice(128 * t, 128 * t + 128)
            uh[rows, cols], ul[rows, cols] = split(u)
            wh[rows, cols], wl[rows, cols] = split(w)
            uth[cols, rows], utl[cols, rows] = split(u.T)
        return carry

    lax.fori_loop(0, 4, pack, 0)

    g_copies = []
    for t, low in ((0, 0), (3, 0), (1, 128), (2, 256)):
        rows = slice(128 * t, 128 * t + 128)
        gram[rows, low:] = dot3((uth[rows, :], utl[rows, :]), (wh[:, low:], wl[:, low:]))
        if t == 0:
            pl.semaphore_wait(barrier, len(partners))
        if t == 3:
            g0[rows_at(core, 64), :] = gram[448:512, :]
            g0_copies = [send(gram.at[pl.ds(448, 64), :], g0.at[rows_at(core, 64), :], other_core)]
        else:
            at = gram.at[pl.ds(128 * t, 128), pl.ds(low, 512 - low)]
            to = g_in.at[pl.ds(128 * t, 128), pl.ds(low, 512 - low)]
            g_copies.append(send(at, to, other_core))
    cap_load.wait()
    halves, eighths = rows_at(core, 64), rows_at(j, 16)
    c1b[lax.div(y, 2)] = cap_v[1]
    c3b[lax.div(x, 2)] = cap_v[3]
    c5b[lax.div(z, 2), eighths, :] = cap_v[5, eighths, :]
    c6b[lax.div(z, 4), eighths, :] = cap_v[6, eighths, :]
    c1_copies = [send(cap_v.at[1, halves, :], c1b.at[lax.div(y, 2), halves, :], y_devices[0])]
    c3_copies = [send(cap_v.at[3, halves, :], c3b.at[lax.div(x, 2), halves, :], x_devices[0])]
    c5_copies = [
        send(cap_v.at[5, eighths, :], c5b.at[lax.div(z, 2), eighths, :], z_devices[r]) for r in (0, 3, 4)
    ]
    c6_copies = [send(cap_v.at[6, eighths, :], c6b.at[lax.div(z, 4), eighths, :], z_devices[0])]

    arrive(g_copies)
    for at, base in ((0, 128), (256, 192)):
        rows = slice(base, base + 64)
        tiles = [gram[rows, low : low + 128] + g_in[rows, low : low + 128] for low in (128, 256, 384)]
        pk[:, at : at + 128] = join(tiles[2], tiles[0])
        pk[:, at + 128 : at + 256] = tiles[1]
    for at, base in ((512, 256), (640, 320)):
        rows = slice(base, base + 64)
        tiles = [gram[rows, low : low + 128] + g_in[rows, low : low + 128] for low in (256, 384)]
        pk[:, at : at + 128] = join(tiles[1], tiles[0])
    pk_in[y] = pk[rows_at(j, 8), :]
    pk_copies = [
        send(pk.at[rows_at(core * 4 + m, 8), :], pk_in.at[y], d) for m, d in zip(y_members, y_devices)
    ]

    for level in range(2):
        rows = pl.ds(pl.multiple_of(64 * level + 32 * core, 32), 32)
        tiles = [gram[rows, low : low + 128] + g_in[rows, low : low + 128] for low in (0, 128, 256, 384)]
        g12[level, :, 0:128] = join(tiles[3], tiles[0])
        g12[level, :, 128:256] = tiles[1]
        g12[level, :, 256:384] = tiles[2]
    core_rows = rows_at(core, 32)
    g1[y, core_rows, :] = g12[0]
    g2r[y, :, :] = g12[1]
    g1_copies = [send(g12.at[0], g1.at[y, core_rows, :], d) for d in y_devices]
    g2_copies = [send(g12.at[1], g2r.at[y], d) for d in y_devices]

    def leaf(c, carry):
        rows = rows_at(c, 512)
        linv_load(c).wait()
        value = dot3(split(linv_v[rows, :]), (oh[...], ol[...]))
        field[0, rows, :] = value[:, :128]
        field[1, rows, :] = value[:, 128:]
        fth[:, rows], ftl[:, rows] = split(value.T)
        return carry

    lax.fori_loop(0, 2, leaf, 0)
    qraw[...] = dot3((fth[...], ftl[...]), (wh[...], wl[...]))

    def update(cols, value):
        width = value.shape[1]
        xh[0:width, 0:256], xl[0:width, 0:256] = split(value.T)

        def step(c, carry):
            rows = rows_at(c, 512)
            taken = dot3((uh[rows, cols], ul[rows, cols]), (xh[0:width, 0:256], xl[0:width, 0:256]))
            field[0, rows, :] = field[0, rows, :] - taken[:, :128]
            field[1, rows, :] = field[1, rows, :] - taken[:, 128:]
            return carry

        lax.fori_loop(0, 2, step, 0)

    own_half = rows_at(core, 128)
    q_copies = [send(qraw.at[rows_at(1 - core, 128), :], q_in, other_core)]
    own_rows = rows_at(j, 8)
    arrive(g0_copies)
    arrive(q_copies)
    arrive(pk_copies)
    x4[x] = pk_in[0] + pk_in[1] + pk_in[2] + pk_in[3]
    x4_copies = [send(x4.at[x], x4.at[x], d) for d in x_devices]
    mine, others = qraw[own_half, :], q_in[...]
    first = jnp.where(core == 0, mine[:, 384:], others[:, 384:])
    second = jnp.where(core == 0, others[:, 384:], mine[:, 384:])
    solved = product(join(swap(second), first), cap_v[0], True)
    q[...] = mine + others - product(solved, g0[...])

    y_in[y] = q[rows_at(y, 32), :]
    y_copies = [send(q.at[rows_at(m, 32), :], y_in.at[y], d) for m, d in zip(y_members, y_devices)]
    swapped = swap(solved)
    z0[0] = solved
    z0[1] = swapped
    z0_copies = [send(z0.at[core], z0.at[2], other_core)]
    arrive(g1_copies)
    arrive(g2_copies)
    g2[0, core_rows, :] = g2r[0] + g2r[1]
    g2[1, core_rows, :] = g2r[2] + g2r[3]
    arrive(c1_copies)
    far1 = 1 - lax.div(y, 2)
    g12c_copies = [
        send(c1b.at[far1, halves, :], c1b.at[far1, halves, :], other_core),
        send(g1.at[:, core_rows, :], g1.at[:, core_rows, :], other_core),
        send(g2.at[:, core_rows, :], g2.at[:, core_rows, :], other_core),
    ]
    arrive(x4_copies)
    for m in range(4):
        mx[m, own_rows, :] = x4[m, :, 0:256]
    for h in range(2):
        mx[4 + h, own_rows, :] = x4[2 * h, :, 256:512] + x4[2 * h + 1, :, 256:512]
    mxy_copies = [send(mx.at[:, own_rows, :], mx.at[:, own_rows, :], d) for d in y_devices]
    z8[z] = x4[0, :, 512:] + x4[1, :, 512:] + x4[2, :, 512:] + x4[3, :, 512:]
    z8_copies = [send(z8.at[z], z8.at[z], d) for d in z_devices]
    arrive(g12c_copies)
    m1 = [jnp.concatenate([g1[2 * n], g1[2 * n + 1]], 0) for n in range(2)]
    m2 = jnp.concatenate([g2[0], g2[1]], 0)
    arrive(y_copies)
    low = [y_in[m, :, 0:128] for m in range(4)]
    z1 = [product(join(low[2 * n + 1], swap(low[2 * n])), c1b[n], True) for n in range(2)]
    y1 = [product(z1[n], m1[n]) for n in range(2)]
    left = [low[2 * h] + low[2 * h + 1] - y1[h][:, :128] for h in range(2)]
    z2 = product(join(swap(left[1]), left[0]), cap_v[2], True)
    taken = y1[0] + y1[1] + product(z2, m2)
    high = y_in[0, :, 128:] + y_in[1, :, 128:] + y_in[2, :, 128:] + y_in[3, :, 128:]
    rr[:, 0:256] = high[:, 0:256] - taken[:, 128:]
    rr[:, 256:384] = high[:, 256:] - taken[:, :128]

    x_in[x] = rr[rows_at(x, 8), :]
    x_copies = [send(rr.at[rows_at(m, 8), :], x_in.at[x], d) for m, d in zip(x_members, x_devices)]
    for m in range(4):
        za[m] = join(put(z1[m // 2], m % 2), put(z2, 1 - m // 2))
    own_cols = rows_at(j, 32)
    zt0[own_cols, :] = za[y]
    za_copies = [send(za.at[m], zt0.at[own_cols, :], d) for m, d in zip(y_members, y_devices)]
    arrive(z8_copies)
    for m in range(8):
        mz[m, own_rows, :] = z8[m, :, 0:128]
    for p in range(4):
        mz[8 + p, own_rows, :] = z8[2 * p, :, 128:] + z8[2 * p + 1, :, 128:]
    mzy_copies = [send(mz.at[:, own_rows, :], mz.at[:, own_rows, :], d) for d in y_devices]
    arrive(c5_copies)
    arrive(c6_copies)
    mzy_copies += [send(c5b.at[:, eighths, :], c5b.at[:, eighths, :], d) for d in y_devices]
    mzy_copies += [send(c6b.at[:, eighths, :], c6b.at[:, eighths, :], d) for d in y_devices]
    arrive(c3_copies)
    arrive(mxy_copies)
    far3 = 1 - lax.div(x, 2)
    mxc_copies = [
        send(mx.at[:, core_rows, :], mx.at[:, core_rows, :], other_core),
        send(c3b.at[far3, halves, :], c3b.at[far3, halves, :], other_core),
    ]
    arrive(mxc_copies)
    m3 = [jnp.concatenate([mx[2 * n], mx[2 * n + 1]], 0) for n in range(2)]
    m4 = jnp.concatenate([mx[4], mx[5]], 0)
    arrive(x_copies)
    low = [x_in[m, :, 0:128] for m in range(4)]
    z3 = [product(join(low[2 * n + 1], swap(low[2 * n])), c3b[n], True) for n in range(2)]
    y3 = [product(z3[n], m3[n]) for n in range(2)]
    left = [low[2 * h] + low[2 * h + 1] - y3[h][:, :128] for h in range(2)]
    z4 = product(join(swap(left[1]), left[0]), cap_v[4], True)
    taken = y3[0] + y3[1] + product(z4, m4)
    high = x_in[0, :, 128:] + x_in[1, :, 128:] + x_in[2, :, 128:] + x_in[3, :, 128:]
    high = jnp.concatenate([high[:, :128] - taken[:, 128:], high[:, 128:] - taken[:, :128]], 1)

    c_in[z] = high
    c_copies = [send(c_in.at[z], c_in.at[z], d) for d in z_devices]
    for m in range(4):
        dx[m] = join(put(z3[m // 2], m % 2), put(z4, 1 - m // 2))
    own_eight = pl.ds(pl.multiple_of(32 * j + 8 * x, 8), 8)
    zt1[own_eight, :] = dx[x]
    zt1_copies = [send(dx.at[m], zt1.at[own_eight, :], d) for m, d in plane_members]
    arrive(mzy_copies)
    mzc_copies = [
        send(mz.at[:, core_rows, :], mz.at[:, core_rows, :], other_core),
        send(c5b.at[:, halves, :], c5b.at[:, halves, :], other_core),
        send(c6b.at[:, halves, :], c6b.at[:, halves, :], other_core),
    ]
    arrive(za_copies)
    half_cols = rows_at(core, 128)
    zac_copies = [send(zt0.at[half_cols, :], zt0.at[half_cols, :], other_core)]
    arrive(mzc_copies)
    m5 = [jnp.concatenate([mz[2 * p], mz[2 * p + 1]], 0) for p in range(4)]
    m6 = [jnp.concatenate([mz[8 + 2 * n], mz[9 + 2 * n]], 0) for n in range(2)]
    arrive(z0_copies)
    arrive(zac_copies)
    near = z0[1 - core]
    far = z0[2]
    own0 = jnp.concatenate([jnp.where(core == 0, near, far), jnp.where(core == 0, far, near)], 0)
    update(slice(0, 128), zt0[...])
    update(slice(384, 512), join(jnp.zeros_like(own0), own0))
    arrive(c_copies)
    low = [c_in[m, :, 0:128] for m in range(8)]
    top = [c_in[m, :, 128:] for m in range(8)]
    z5 = [product(join(low[2 * p + 1], swap(low[2 * p])), c5b[p], True) for p in range(4)]
    y5 = [product(z5[p], m5[p]) for p in range(4)]
    left = [low[2 * p] + low[2 * p + 1] - y5[p] for p in range(4)]
    z6 = [product(join(swap(left[2 * n + 1]), left[2 * n]), c6b[n], True) for n in range(2)]
    y6 = [product(z6[n], m6[n]) for n in range(2)]
    left = []
    for h in range(2):
        value = top[4 * h] + top[4 * h + 1] + top[4 * h + 2] + top[4 * h + 3]
        left.append(value - y5[2 * h] - y5[2 * h + 1] - y6[h])
    z7 = product(join(left[1], swap(left[0])), cap_v[7], True)
    for p in range(4):
        z5s[p] = z5[p]
    for n in range(2):
        z6s[n] = z6[n]
    side5, side6, side7 = lax.rem(z, 2), lax.rem(lax.div(z, 2), 2), lax.div(z, 4)
    own5 = z5s[lax.div(z, 2)]
    own5 = jnp.where(side5 == 0, own5, swap(own5))
    own6 = z6s[lax.div(z, 4)]
    own6 = jnp.where(side6 == 0, swap(own6), own6)
    own7 = jnp.where(side7 == 0, z7, swap(z7))
    last = jnp.concatenate([join(own5, own6), join(own7, jnp.zeros_like(own7))], 1)

    d_out[...] = last
    ztb[own_eight, :] = last
    ztb_copies = [send(d_out, ztb.at[own_eight, :], d) for _, d in plane_members]
    arrive(zt1_copies)
    zt1c_copies = [send(zt1.at[half_cols, :], zt1.at[half_cols, :], other_core)]
    arrive(zt1c_copies)
    update(slice(128, 256), zt1[...])
    arrive(ztb_copies)
    ztbc_copies = [send(ztb.at[half_cols, :], ztb.at[half_cols, :], other_core)]
    arrive(ztbc_copies)
    update(slice(256, 512), ztb[...])
    for copy in started:
        copy.wait_send()
    assert used[0] == COPIES


def scatter_kernel(field, order, out, high, low, done, sems):
    local = order[...] - lax.axis_index("rows") * 512
    for c in range(2):
        value = jnp.concatenate([field[h, pl.ds(c, 512, stride=2), :] for h in range(2)], 1)
        high[:, 256 * c : 256 * c + 256], low[:, 256 * c : 256 * c + 256] = split(value)
    copies = []
    for b in range(4):
        pick = one_hot(local, 128 * b, 128).astype(BF16)
        moved = mm(pick, high[...]) + mm(pick, low[...])
        for c in range(2):
            for h in range(2):
                at = 256 * c + 128 * h
                done[pl.ds(512 * b + 2 * h + c, 128, stride=4), :] = moved[:, at : at + 128]
        rows = pl.ds(512 * b, 512)
        copies.append(pltpu.make_async_copy(done.at[rows, :], out.at[rows, :], sems.at[b]))
        copies[-1].start()
    for copy in copies:
        copy.wait()


def shards(right_sides, order, leaf_inverse, basis, capacitance):
    rhs = right_sides.reshape(512, 2, 2, 128).transpose(0, 2, 1, 3).reshape(2048, 128)
    order = order.reshape(1, 512)
    any_ref = pl.BlockSpec(memory_space=pl.ANY)
    vmem_ref = pl.BlockSpec(memory_space=pltpu.VMEM)
    f, h = (lambda *shape: pltpu.VMEM(shape, F32)), (lambda *shape: pltpu.VMEM(shape, BF16))
    field = pl.pallas_call(
        solve_kernel,
        out_shape=pltpu.VMEM((2, 1024, 128), F32),
        in_specs=[any_ref, vmem_ref, any_ref, any_ref, any_ref],
        out_specs=vmem_ref,
        scratch_shapes=[
            f(2048, 128), f(1024, 1024), f(8, 1024, 128), f(8, 128, 128),
            h(1024, 512), h(1024, 512), h(1024, 512), h(1024, 512),
            h(512, 1024), h(512, 1024), h(256, 1024), h(256, 1024), f(512, 512),
            h(512, 512), h(512, 512), h(512, 512), f(2, 1024, 128),
            h(1024, 256), h(1024, 256),
            f(256, 512), f(128, 512), f(128, 512), f(4, 32, 512), f(4, 32, 128), f(3, 128, 128),
            f(32, 384), f(4, 8, 384), f(8, 8, 256), f(4, 8, 128), f(2, 8, 128), f(4, 8, 128),
            f(8, 256), f(256, 128), f(256, 128), f(256, 256),
            f(2, 128, 128), f(2, 128, 128), f(4, 128, 128), f(2, 128, 128),
            f(512, 512), f(128, 512), f(2, 32, 384), f(4, 64, 384), f(4, 32, 384), f(2, 64, 384),
            f(64, 768), f(4, 8, 768), f(4, 8, 768), f(8, 8, 256), f(6, 64, 256), f(12, 64, 128),
            pltpu.SemaphoreType.DMA((COPIES,)), pltpu.SemaphoreType.DMA((COPIES,)),
            pltpu.SemaphoreType.DMA((22,)),
        ],
        compiler_params=pltpu.CompilerParams(
            collective_id=0, has_side_effects=True, vmem_limit_bytes=VMEM_BYTES
        ),
    )(rhs, order, leaf_inverse, basis, capacitance.reshape(8, 128, 128))
    out = pl.pallas_call(
        scatter_kernel,
        out_shape=jax.ShapeDtypeStruct((2048, 128), F32),
        in_specs=[vmem_ref, vmem_ref],
        out_specs=any_ref,
        scratch_shapes=[h(512, 512), h(512, 512), f(2048, 128), pltpu.SemaphoreType.DMA((4,))],
        compiler_params=pltpu.CompilerParams(vmem_limit_bytes=16 * 1024 * 1024),
    )(field, order)
    return out.reshape(512, 2, 2, 128).transpose(0, 2, 1, 3).reshape(512, 2, 256)


def solution(mesh):
    return jax.shard_map(
        shards,
        mesh=mesh,
        in_specs=(
            P("rows", None, None),
            P("rows"),
            P("rows", None),
            P(None, "rows", None),
            P(None, "rows", None, None),
        ),
        out_specs=P("rows", None, None),
        check_vma=False,
    )
```

```python
import functools

import jax
import jax.numpy as jnp
from jax import lax
from jax.experimental import pallas as pl
from jax.experimental.pallas import tpu as pltpu
from jax.sharding import PartitionSpec as P

F32 = jnp.float32
BF16 = jnp.bfloat16
MESH = pl.DeviceIdType.MESH
PACKED = (1, 2, 3, 4, 5, 6, 7, 0)
COPIES = 100
VMEM_BYTES = 58 * 1024 * 1024


def split(x):
    high = x.astype(BF16)
    return high, (x - high.astype(F32)).astype(BF16)


def mm(a, b, transposed=False):
    return lax.dot_general(
        a, b, (((1,), (1 if transposed else 0,)), ((), ())), preferred_element_type=F32
    )


def dot3(a, b, transposed=False):
    return mm(a[0], b[0], transposed) + (
        mm(a[0], b[1], transposed) + mm(a[1], b[0], transposed)
    )


def product(a, b, transposed=False):
    return dot3(split(a), split(b), transposed)


def lanes_of(x):
    return lax.broadcasted_iota(jnp.int32, x.shape, 1)


def swap(x):
    return pltpu.roll(x, 64, 1)


def join(left, right):
    return jnp.where(lanes_of(left) < 64, left, right)


def put(half, side):
    return half if side == 0 else swap(half)


def one_hot(order, first, count):
    rows = lax.broadcasted_iota(jnp.int32, (count, order.shape[1]), 0) + first
    return jnp.where(rows == order, 1.0, 0.0)


def solve_kernel(
    rhs, order, linv, basis, cap,
    field,
    rhs_v, linv_v, basis_v, cap_v,
    uh, ul, wh, wl, uth, utl, fth, ftl, gram,
    pick, xh, xl, gathered, oh, ol,
    qraw, q_in, q, y_in, za, z0, rr, x_in, c_in, z5s, z6s, dx, d_out, zt0, zt1, ztb,
    c1b, c3b, c5b, c6b, g_in, g0, g12, g1, g2r, g2, pk, pk_in, x4, z8, mx, mz,
    ssem, rsem, lsem,
):
    me = lax.axis_index("rows")
    core = lax.rem(me, 2)
    y = lax.rem(lax.div(me, 2), 4)
    x = lax.rem(lax.div(me, 8), 4)
    z = lax.div(me, 32)
    j = core * 4 + y
    plane = z * 32
    row = plane + x * 8
    cell = y * 2 + core

    y_members = [lax.rem(y + r, 4) for r in (2, 1, 3)]
    y_devices = [row + m * 2 + core for m in y_members]
    x_members = [lax.rem(x + r, 4) for r in (2, 1, 3)]
    x_devices = [plane + m * 8 + cell for m in x_members]
    z_members = [lax.rem(z + r, 8) for r in (4, 3, 5, 2, 6, 1, 7)]
    z_devices = [m * 32 + x * 8 + cell for m in z_members]
    other_core = row + y * 2 + (1 - core)
    plane_members = []
    for dy, dx_ in ((2, 2), (2, 1), (2, 3), (1, 2), (3, 2), (1, 1), (1, 3), (3, 1), (3, 3), (2, 0), (0, 2), (1, 0), (3, 0), (0, 1), (0, 3)):
        other_y, other_x = lax.rem(y + dy, 4), lax.rem(x + dx_, 4)
        plane_members.append((other_x, plane + other_x * 8 + other_y * 2 + core))

    def rows_at(index, count):
        return pl.ds(pl.multiple_of(index * count, count), count)

    used = [0]
    started = []

    def send(src, dst, device):
        at = used[0]
        used[0] += 1
        copy = pltpu.make_async_remote_copy(
            src_ref=src,
            dst_ref=dst,
            send_sem=ssem.at[at],
            recv_sem=rsem.at[at],
            device_id=(device,),
            device_id_type=MESH,
        )
        copy.start()
        started.append(copy)
        return copy

    def arrive(copies):
        for copy in copies:
            copy.wait_recv()

    def basis_load(c):
        rows = pl.ds(c * 256, 256)
        return pltpu.make_async_copy(basis.at[:, rows, :], basis_v.at[:, rows, :], lsem.at[c])

    def linv_load(c):
        rows = pl.ds(c * 512, 512)
        return pltpu.make_async_copy(linv.at[rows, :], linv_v.at[rows, :], lsem.at[8 + c])

    for c in range(4):
        basis_load(c).start()
    cap_load = pltpu.make_async_copy(cap, cap_v, lsem.at[16])
    cap_load.start()
    rhs_load = pltpu.make_async_copy(rhs, rhs_v, lsem.at[17])

    barrier = pltpu.get_barrier_semaphore()
    partners = [other_core] + [d for _, d in plane_members] + z_devices
    for device in partners:
        pl.semaphore_signal(barrier, inc=1, device_id=(device,), device_id_type=MESH)

    def pack(c, carry):
        rows = rows_at(c, 256)
        basis_load(c).wait()

        @pl.when(c == 2)
        def _():
            rhs_load.start()

        @pl.when(c == 3)
        def _():
            for part in range(2):
                linv_load(part).start()

        for t in range(4):
            a = basis_v[PACKED[2 * t], rows, :]
            b = basis_v[PACKED[2 * t + 1], rows, :]
            u = join(a, swap(b))
            w = join(swap(a), b)
            cols = slice(128 * t, 128 * t + 128)
            uh[rows, cols], ul[rows, cols] = split(u)
            wh[rows, cols], wl[rows, cols] = split(w)
            uth[cols, rows], utl[cols, rows] = split(u.T)
        return carry

    lax.fori_loop(0, 4, pack, 0)

    pl.semaphore_wait(barrier, len(partners))
    cap_load.wait()
    halves, eighths = rows_at(core, 64), rows_at(j, 16)
    c1b[lax.div(y, 2)] = cap_v[1]
    c3b[lax.div(x, 2)] = cap_v[3]
    c5b[lax.div(z, 2), eighths, :] = cap_v[5, eighths, :]
    c6b[lax.div(z, 4), eighths, :] = cap_v[6, eighths, :]
    c1_copies = [send(cap_v.at[1, halves, :], c1b.at[lax.div(y, 2), halves, :], y_devices[0])]
    c3_copies = [send(cap_v.at[3, halves, :], c3b.at[lax.div(x, 2), halves, :], x_devices[0])]
    c5_copies = [
        send(cap_v.at[5, eighths, :], c5b.at[lax.div(z, 2), eighths, :], z_devices[r]) for r in (0, 3, 4)
    ]
    c6_copies = [send(cap_v.at[6, eighths, :], c6b.at[lax.div(z, 4), eighths, :], z_devices[0])]

    g_copies = []
    for t, low in ((0, 0), (3, 0), (1, 128), (2, 256)):
        rows = slice(128 * t, 128 * t + 128)
        gram[rows, low:] = dot3((uth[rows, :], utl[rows, :]), (wh[:, low:], wl[:, low:]))
        if t == 3:
            g0[rows_at(core, 64), :] = gram[448:512, :]
            g0_copies = [send(gram.at[pl.ds(448, 64), :], g0.at[rows_at(core, 64), :], other_core)]
        else:
            at = gram.at[pl.ds(128 * t, 128), pl.ds(low, 512 - low)]
            to = g_in.at[pl.ds(128 * t, 128), pl.ds(low, 512 - low)]
            g_copies.append(send(at, to, other_core))
    rhs_load.wait()
    local = order[...] - me * 512
    for b in range(4):
        pick[:, 128 * b : 128 * b + 128] = one_hot(local, 128 * b, 128).T.astype(BF16)
    for c in range(2):
        for half in range(2):
            cols = slice((2 * c + half) * 128, (2 * c + half) * 128 + 128)
            xh[:, cols], xl[:, cols] = split(rhs_v[pl.ds(2 * half + c, 512, stride=4), :])

    arrive(g_copies)
    for at, base in ((0, 128), (256, 192)):
        rows = slice(base, base + 64)
        tiles = [gram[rows, low : low + 128] + g_in[rows, low : low + 128] for low in (128, 256, 384)]
        pk[:, at : at + 128] = join(tiles[2], tiles[0])
        pk[:, at + 128 : at + 256] = tiles[1]
    for at, base in ((512, 256), (640, 320)):
        rows = slice(base, base + 64)
        tiles = [gram[rows, low : low + 128] + g_in[rows, low : low + 128] for low in (256, 384)]
        pk[:, at : at + 128] = join(tiles[1], tiles[0])
    pk_in[y] = pk[rows_at(j, 8), :]
    pk_copies = [
        send(pk.at[rows_at(core * 4 + m, 8), :], pk_in.at[y], d) for m, d in zip(y_members, y_devices)
    ]

    for level in range(2):
        rows = pl.ds(pl.multiple_of(64 * level + 32 * core, 32), 32)
        tiles = [gram[rows, low : low + 128] + g_in[rows, low : low + 128] for low in (0, 128, 256, 384)]
        g12[level, :, 0:128] = join(tiles[3], tiles[0])
        g12[level, :, 128:256] = tiles[1]
        g12[level, :, 256:384] = tiles[2]
    core_rows = rows_at(core, 32)
    g1[y, core_rows, :] = g12[0]
    g2r[y, :, :] = g12[1]
    g1_copies = [send(g12.at[0], g1.at[y, core_rows, :], d) for d in y_devices]
    g2_copies = [send(g12.at[1], g2r.at[y], d) for d in y_devices]

    for source, target in ((xh, oh), (xl, ol)):
        for b in range(4):
            moved = mm(pick[128 * b : 128 * b + 128, :], source[...])
            for c in range(2):
                for half in range(2):
                    at = (2 * c + half) * 128
                    gathered[half, pl.ds(256 * b + c, 128, stride=2), :] = moved[:, at : at + 128]
        for half in range(2):
            target[:, 128 * half : 128 * half + 128] = gathered[half].astype(BF16)

    def leaf(c, carry):
        rows = rows_at(c, 512)
        linv_load(c).wait()
        value = dot3(split(linv_v[rows, :]), (oh[...], ol[...]))
        field[0, rows, :] = value[:, :128]
        field[1, rows, :] = value[:, 128:]
        fth[:, rows], ftl[:, rows] = split(value.T)
        return carry

    lax.fori_loop(0, 2, leaf, 0)
    qraw[...] = dot3((fth[...], ftl[...]), (wh[...], wl[...]))

    def update(cols, value):
        width = value.shape[1]
        xh[0:width, 0:256], xl[0:width, 0:256] = split(value.T)

        def step(c, carry):
            rows = rows_at(c, 512)
            taken = dot3((uh[rows, cols], ul[rows, cols]), (xh[0:width, 0:256], xl[0:width, 0:256]))
            field[0, rows, :] = field[0, rows, :] - taken[:, :128]
            field[1, rows, :] = field[1, rows, :] - taken[:, 128:]
            return carry

        lax.fori_loop(0, 2, step, 0)

    own_half = rows_at(core, 128)
    q_copies = [send(qraw.at[rows_at(1 - core, 128), :], q_in, other_core)]
    own_rows = rows_at(j, 8)
    arrive(g0_copies)
    arrive(q_copies)
    arrive(pk_copies)
    x4[x] = pk_in[0] + pk_in[1] + pk_in[2] + pk_in[3]
    x4_copies = [send(x4.at[x], x4.at[x], d) for d in x_devices]
    mine, others = qraw[own_half, :], q_in[...]
    first = jnp.where(core == 0, mine[:, 384:], others[:, 384:])
    second = jnp.where(core == 0, others[:, 384:], mine[:, 384:])
    solved = product(join(swap(second), first), cap_v[0], True)
    q[...] = mine + others - product(solved, g0[...])

    y_in[y] = q[rows_at(y, 32), :]
    y_copies = [send(q.at[rows_at(m, 32), :], y_in.at[y], d) for m, d in zip(y_members, y_devices)]
    swapped = swap(solved)
    z0[0] = solved
    z0[1] = swapped
    z0_copies = [send(z0.at[core], z0.at[2], other_core)]
    arrive(g1_copies)
    arrive(g2_copies)
    g2[0, core_rows, :] = g2r[0] + g2r[1]
    g2[1, core_rows, :] = g2r[2] + g2r[3]
    arrive(c1_copies)
    far1 = 1 - lax.div(y, 2)
    g12c_copies = [
        send(c1b.at[far1, halves, :], c1b.at[far1, halves, :], other_core),
        send(g1.at[:, core_rows, :], g1.at[:, core_rows, :], other_core),
        send(g2.at[:, core_rows, :], g2.at[:, core_rows, :], other_core),
    ]
    arrive(x4_copies)
    for m in range(4):
        mx[m, own_rows, :] = x4[m, :, 0:256]
    for h in range(2):
        mx[4 + h, own_rows, :] = x4[2 * h, :, 256:512] + x4[2 * h + 1, :, 256:512]
    mxy_copies = [send(mx.at[:, own_rows, :], mx.at[:, own_rows, :], d) for d in y_devices]
    z8[z] = x4[0, :, 512:] + x4[1, :, 512:] + x4[2, :, 512:] + x4[3, :, 512:]
    z8_copies = [send(z8.at[z], z8.at[z], d) for d in z_devices]
    arrive(g12c_copies)
    m1 = [jnp.concatenate([g1[2 * n], g1[2 * n + 1]], 0) for n in range(2)]
    m2 = jnp.concatenate([g2[0], g2[1]], 0)
    arrive(y_copies)
    low = [y_in[m, :, 0:128] for m in range(4)]
    z1 = [product(join(low[2 * n + 1], swap(low[2 * n])), c1b[n], True) for n in range(2)]
    y1 = [product(z1[n], m1[n]) for n in range(2)]
    left = [low[2 * h] + low[2 * h + 1] - y1[h][:, :128] for h in range(2)]
    z2 = product(join(swap(left[1]), left[0]), cap_v[2], True)
    taken = y1[0] + y1[1] + product(z2, m2)
    high = y_in[0, :, 128:] + y_in[1, :, 128:] + y_in[2, :, 128:] + y_in[3, :, 128:]
    rr[:, 0:256] = high[:, 0:256] - taken[:, 128:]
    rr[:, 256:384] = high[:, 256:] - taken[:, :128]

    x_in[x] = rr[rows_at(x, 8), :]
    x_copies = [send(rr.at[rows_at(m, 8), :], x_in.at[x], d) for m, d in zip(x_members, x_devices)]
    for m in range(4):
        za[m] = join(put(z1[m // 2], m % 2), put(z2, 1 - m // 2))
    own_cols = rows_at(j, 32)
    zt0[own_cols, :] = za[y]
    za_copies = [send(za.at[m], zt0.at[own_cols, :], d) for m, d in zip(y_members, y_devices)]
    arrive(z8_copies)
    for m in range(8):
        mz[m, own_rows, :] = z8[m, :, 0:128]
    for p in range(4):
        mz[8 + p, own_rows, :] = z8[2 * p, :, 128:] + z8[2 * p + 1, :, 128:]
    mzy_copies = [send(mz.at[:, own_rows, :], mz.at[:, own_rows, :], d) for d in y_devices]
    arrive(c5_copies)
    arrive(c6_copies)
    mzy_copies += [send(c5b.at[:, eighths, :], c5b.at[:, eighths, :], d) for d in y_devices]
    mzy_copies += [send(c6b.at[:, eighths, :], c6b.at[:, eighths, :], d) for d in y_devices]
    arrive(c3_copies)
    arrive(mxy_copies)
    far3 = 1 - lax.div(x, 2)
    mxc_copies = [
        send(mx.at[:, core_rows, :], mx.at[:, core_rows, :], other_core),
        send(c3b.at[far3, halves, :], c3b.at[far3, halves, :], other_core),
    ]
    arrive(mxc_copies)
    m3 = [jnp.concatenate([mx[2 * n], mx[2 * n + 1]], 0) for n in range(2)]
    m4 = jnp.concatenate([mx[4], mx[5]], 0)
    arrive(x_copies)
    low = [x_in[m, :, 0:128] for m in range(4)]
    z3 = [product(join(low[2 * n + 1], swap(low[2 * n])), c3b[n], True) for n in range(2)]
    y3 = [product(z3[n], m3[n]) for n in range(2)]
    left = [low[2 * h] + low[2 * h + 1] - y3[h][:, :128] for h in range(2)]
    z4 = product(join(swap(left[1]), left[0]), cap_v[4], True)
    taken = y3[0] + y3[1] + product(z4, m4)
    high = x_in[0, :, 128:] + x_in[1, :, 128:] + x_in[2, :, 128:] + x_in[3, :, 128:]
    high = jnp.concatenate([high[:, :128] - taken[:, 128:], high[:, 128:] - taken[:, :128]], 1)

    c_in[z] = high
    c_copies = [send(c_in.at[z], c_in.at[z], d) for d in z_devices]
    for m in range(4):
        dx[m] = join(put(z3[m // 2], m % 2), put(z4, 1 - m // 2))
    own_eight = pl.ds(pl.multiple_of(32 * j + 8 * x, 8), 8)
    zt1[own_eight, :] = dx[x]
    zt1_copies = [send(dx.at[m], zt1.at[own_eight, :], d) for m, d in plane_members]
    arrive(mzy_copies)
    mzc_copies = [
        send(mz.at[:, core_rows, :], mz.at[:, core_rows, :], other_core),
        send(c5b.at[:, halves, :], c5b.at[:, halves, :], other_core),
        send(c6b.at[:, halves, :], c6b.at[:, halves, :], other_core),
    ]
    arrive(za_copies)
    half_cols = rows_at(core, 128)
    zac_copies = [send(zt0.at[half_cols, :], zt0.at[half_cols, :], other_core)]
    arrive(mzc_copies)
    m5 = [jnp.concatenate([mz[2 * p], mz[2 * p + 1]], 0) for p in range(4)]
    m6 = [jnp.concatenate([mz[8 + 2 * n], mz[9 + 2 * n]], 0) for n in range(2)]
    arrive(z0_copies)
    arrive(zac_copies)
    near = z0[1 - core]
    far = z0[2]
    own0 = jnp.concatenate([jnp.where(core == 0, near, far), jnp.where(core == 0, far, near)], 0)
    update(slice(0, 128), zt0[...])
    update(slice(384, 512), join(jnp.zeros_like(own0), own0))
    arrive(c_copies)
    low = [c_in[m, :, 0:128] for m in range(8)]
    top = [c_in[m, :, 128:] for m in range(8)]
    z5 = [product(join(low[2 * p + 1], swap(low[2 * p])), c5b[p], True) for p in range(4)]
    y5 = [product(z5[p], m5[p]) for p in range(4)]
    left = [low[2 * p] + low[2 * p + 1] - y5[p] for p in range(4)]
    z6 = [product(join(swap(left[2 * n + 1]), left[2 * n]), c6b[n], True) for n in range(2)]
    y6 = [product(z6[n], m6[n]) for n in range(2)]
    left = []
    for h in range(2):
        value = top[4 * h] + top[4 * h + 1] + top[4 * h + 2] + top[4 * h + 3]
        left.append(value - y5[2 * h] - y5[2 * h + 1] - y6[h])
    z7 = product(join(left[1], swap(left[0])), cap_v[7], True)
    for p in range(4):
        z5s[p] = z5[p]
    for n in range(2):
        z6s[n] = z6[n]
    side5, side6, side7 = lax.rem(z, 2), lax.rem(lax.div(z, 2), 2), lax.div(z, 4)
    own5 = z5s[lax.div(z, 2)]
    own5 = jnp.where(side5 == 0, own5, swap(own5))
    own6 = z6s[lax.div(z, 4)]
    own6 = jnp.where(side6 == 0, swap(own6), own6)
    own7 = jnp.where(side7 == 0, z7, swap(z7))
    last = jnp.concatenate([join(own5, own6), join(own7, jnp.zeros_like(own7))], 1)

    d_out[...] = last
    ztb[own_eight, :] = last
    ztb_copies = [send(d_out, ztb.at[own_eight, :], d) for _, d in plane_members]
    arrive(zt1_copies)
    zt1c_copies = [send(zt1.at[half_cols, :], zt1.at[half_cols, :], other_core)]
    arrive(zt1c_copies)
    update(slice(128, 256), zt1[...])
    arrive(ztb_copies)
    ztbc_copies = [send(ztb.at[half_cols, :], ztb.at[half_cols, :], other_core)]
    arrive(ztbc_copies)
    update(slice(256, 512), ztb[...])
    for copy in started:
        copy.wait_send()
    assert used[0] == COPIES


def scatter_kernel(field, order, out, high, low, done, sems):
    local = order[...] - lax.axis_index("rows") * 512
    for c in range(2):
        value = jnp.concatenate([field[h, pl.ds(c, 512, stride=2), :] for h in range(2)], 1)
        high[:, 256 * c : 256 * c + 256], low[:, 256 * c : 256 * c + 256] = split(value)
    copies = []
    for b in range(4):
        pick = one_hot(local, 128 * b, 128).astype(BF16)
        moved = mm(pick, high[...]) + mm(pick, low[...])
        for c in range(2):
            for h in range(2):
                at = 256 * c + 128 * h
                done[pl.ds(512 * b + 2 * h + c, 128, stride=4), :] = moved[:, at : at + 128]
        rows = pl.ds(512 * b, 512)
        copies.append(pltpu.make_async_copy(done.at[rows, :], out.at[rows, :], sems.at[b]))
        copies[-1].start()
    for copy in copies:
        copy.wait()


def shards(right_sides, order, leaf_inverse, basis, capacitance):
    rhs = right_sides.reshape(512, 2, 2, 128).transpose(0, 2, 1, 3).reshape(2048, 128)
    order = order.reshape(1, 512)
    any_ref = pl.BlockSpec(memory_space=pl.ANY)
    vmem_ref = pl.BlockSpec(memory_space=pltpu.VMEM)
    f, h = (lambda *shape: pltpu.VMEM(shape, F32)), (lambda *shape: pltpu.VMEM(shape, BF16))
    field = pl.pallas_call(
        solve_kernel,
        out_shape=pltpu.VMEM((2, 1024, 128), F32),
        in_specs=[any_ref, vmem_ref, any_ref, any_ref, any_ref],
        out_specs=vmem_ref,
        scratch_shapes=[
            f(2048, 128), f(1024, 1024), f(8, 1024, 128), f(8, 128, 128),
            h(1024, 512), h(1024, 512), h(1024, 512), h(1024, 512),
            h(512, 1024), h(512, 1024), h(256, 1024), h(256, 1024), f(512, 512),
            h(512, 512), h(512, 512), h(512, 512), f(2, 1024, 128),
            h(1024, 256), h(1024, 256),
            f(256, 512), f(128, 512), f(128, 512), f(4, 32, 512), f(4, 32, 128), f(3, 128, 128),
            f(32, 384), f(4, 8, 384), f(8, 8, 256), f(4, 8, 128), f(2, 8, 128), f(4, 8, 128),
            f(8, 256), f(256, 128), f(256, 128), f(256, 256),
            f(2, 128, 128), f(2, 128, 128), f(4, 128, 128), f(2, 128, 128),
            f(512, 512), f(128, 512), f(2, 32, 384), f(4, 64, 384), f(4, 32, 384), f(2, 64, 384),
            f(64, 768), f(4, 8, 768), f(4, 8, 768), f(8, 8, 256), f(6, 64, 256), f(12, 64, 128),
            pltpu.SemaphoreType.DMA((COPIES,)), pltpu.SemaphoreType.DMA((COPIES,)),
            pltpu.SemaphoreType.DMA((22,)),
        ],
        compiler_params=pltpu.CompilerParams(
            collective_id=0, has_side_effects=True, vmem_limit_bytes=VMEM_BYTES
        ),
    )(rhs, order, leaf_inverse, basis, capacitance.reshape(8, 128, 128))
    out = pl.pallas_call(
        scatter_kernel,
        out_shape=jax.ShapeDtypeStruct((2048, 128), F32),
        in_specs=[vmem_ref, vmem_ref],
        out_specs=any_ref,
        scratch_shapes=[h(512, 512), h(512, 512), f(2048, 128), pltpu.SemaphoreType.DMA((4,))],
        compiler_params=pltpu.CompilerParams(vmem_limit_bytes=16 * 1024 * 1024),
    )(field, order)
    return out.reshape(512, 2, 2, 128).transpose(0, 2, 1, 3).reshape(512, 2, 256)


def solution(mesh):
    return jax.shard_map(
        shards,
        mesh=mesh,
        in_specs=(
            P("rows", None, None),
            P("rows"),
            P("rows", None),
            P(None, "rows", None),
            P(None, "rows", None, None),
        ),
        out_specs=P("rows", None, None),
        check_vma=False,
    )
```
